128 devices in a mesh: seq: 128 (over x, z, y, core).
Axes of the slice: x: 4, y: 4, z: 4, core: 2. Of those that a mesh axis runs over, the one named last changes fastest.
Arguments:
- acceptance_gate: bfloat16 [16384, 2048], P('seq'), may hold values from -1.1953125 to 1.1953125
- lookup_matrix: bfloat16 [16384, 2048], P('seq'), may hold values from -0.29882812 to 0.29882812
- payload_matrix: bfloat16 [16384, 2048], P('seq'), may hold values from -6 to 6
- fading_parameter: float32 [16384, 2048], P('seq'), may hold values from -17 to 0.5
- present_reward: float32 [2048], replicated, may hold values from -4 to 4
- emitted_cotangent: bfloat16 [16384, 2048], P('seq'), may hold values from -0.119628906 to 0.119628906
- paper_spans: int32 [256], replicated, may hold values from 1 to 4096, 16384 in all
Outputs:
- grad_receptance: bfloat16 [16384, 2048], P('seq')
- grad_key: bfloat16 [16384, 2048], P('seq')
- grad_value: bfloat16 [16384, 2048], P('seq')
- grad_decay: bfloat16 [16384, 2048], P('seq')
- reward_cotangent: float32 [2048], replicated
The draws below stay inside these ranges and needn't reach their ends.
Inputs may be any that keep to these rules, and one draw needn't show every extreme that they name: `paper_spans`: the 256 documents fill the packed sequence of 16384 tokens in order.
All inputs are finite; a program needn't handle non-finite values.
Results may differ from the reference program's by a relative error of at most 0.001.
Values sent between devices are 32-bit elements; how exact they have to be, the bound alone decides.
No kernel may reach another device: no remote copies, remote signals or barrier semaphores. Data moves between devices by JAX's collectives and lax.ppermute only.
A program may use at most 320 MiB of HBM per device.

```python
import math
import jax
import jax.numpy as jnp
import numpy as np
from jax import lax

HEADS = 32
HS = 64
BL = 128
TOK_DEV = 128
FEATURE_DIM = 2048
TOKENS = 16384
NDOCS = 256


def draw_fading_parameter(key, part):
    keys = jax.random.split(jax.random.fold_in(key, 17), 7)
    share = 0.5
    quick = jax.random.uniform(keys[0], (HEADS, 1)) < share
    fast_rate = jnp.exp(jax.random.uniform(keys[1], (HEADS, HS), jnp.float32, math.log(math.log(10.0) / 50.0), math.log(math.log(10.0) / 30.0)))
    slow_rate = jnp.exp(jax.random.uniform(keys[2], (HEADS, HS), jnp.float32, math.log(math.log(10.0) / (40.0 * TOKENS)), math.log(math.log(10.0) / (4.0 * TOKENS))))
    starting_displacement = jnp.where(quick, fast_rate, slow_rate).reshape(1, FEATURE_DIM)
    splitting_multiplier = jnp.exp(jax.random.uniform(keys[3], (TOKENS // TOK_DEV, 1, FEATURE_DIM), jnp.float32, -math.log(2.0), math.log(2.0)))
    splitting_multiplier = jnp.broadcast_to(splitting_multiplier, (TOKENS // TOK_DEV, TOK_DEV, FEATURE_DIM)).reshape(TOKENS, FEATURE_DIM)
    approximate_guess = jnp.exp(jax.random.uniform(keys[4], (TOKENS, FEATURE_DIM), jnp.float32, -math.log(2.0), math.log(2.0)))
    arrangement_sequence = jax.random.randint(keys[5], (3,), 0, TOKENS)
    displacement_offsets = jax.random.uniform(keys[6], (3,), jnp.float32, 0.22, 0.69)
    symbol_total = jnp.arange(TOKENS)
    cluster_batch = jnp.sum(jnp.where(symbol_total[:, None] == arrangement_sequence[None, :], displacement_offsets[None, :], 0.0), axis=1)
    fading_speed = starting_displacement * splitting_multiplier * approximate_guess + cluster_batch[:, None]
    return jnp.log(fading_speed).astype(jnp.float32)


def block_scale(rng, shape, shards, smallest, top_value):
    factor_of, own = 1.0, jax.random.fold_in(rng, 6)
    for dim, shards_of in shards:
        draws = jnp.exp(jax.random.uniform(jax.random.fold_in(own, dim), (shards_of,), jnp.float32, smallest / len(shards), top_value / len(shards)))
        factor_of = factor_of * jnp.repeat(draws, shape[dim] // shards_of).reshape([-1 if axis == dim else 1 for axis in range(len(shape))])
    return factor_of


def split_up(count, total, most, lean):
    loads = [(1 << 20) // math.isqrt(rank ** lean) + 1 for rank in range(2, count + 1)]
    spare, counts = total - most - (count - 1), [1] * (count - 1)
    while spare > 0:
        free = [i for i in range(count - 1) if counts[i] < most]
        pool, budget = sum([loads[i] for i in free]), spare
        for i in free:
            more = min(most - counts[i], max(1, budget * loads[i] // pool), spare)
            counts[i] = counts[i] + more
            spare = spare - more
    return np.array([most] + counts)


def ragged(rng, amount, total, limit, skew):
    if amount == 2:
        one = jax.random.randint(rng, (), max(1, total - limit), min(limit, total - 1) + 1)
        return jnp.stack([one, total - one])
    tallies = jnp.asarray(split_up(amount, total, limit, skew), jnp.int32)
    pairs = (amount - 1) // 2
    source_of, taker = tallies[1:1 + 2 * pairs:2], tallies[2:2 + 2 * pairs:2]
    margin = jnp.minimum(source_of - 1, limit - taker)
    shifted = jax.random.randint(jax.random.fold_in(rng, 1), (pairs,), 0, 1 << 20) % (margin + 1)
    tallies = tallies.at[1:1 + 2 * pairs:2].set(source_of - shifted).at[2:2 + 2 * pairs:2].set(taker + shifted)
    return tallies[jax.random.permutation(jax.random.fold_in(rng, 2), amount)]


def centred(stream_key, dims, deviation, most, shards=(), held_as=jnp.bfloat16):
    result = deviation * jax.random.normal(stream_key, dims, jnp.float32)
    if shards:
        result = result * block_scale(stream_key, dims, shards, -0.22, 0.18)
    return jnp.clip(result, -most, most).astype(held_as)


def setup_inputs(seed: int = 0) -> dict:
    splits = jax.random.split(jax.random.key(seed), 8)
    return {
        "acceptance_gate": centred(splits[0], (TOKENS, FEATURE_DIM), 0.2, 1.1953125, ((0, 128),)),
        "lookup_matrix": centred(splits[1], (TOKENS, FEATURE_DIM), 0.05, 0.29882812, ((0, 128),)),
        "payload_matrix": centred(splits[2], (TOKENS, FEATURE_DIM), 1.0, 6.0, ((0, 128),)),
        "fading_parameter": draw_fading_parameter(jax.random.fold_in(splits[7], 71), 0),
        "present_reward": centred(splits[4], (FEATURE_DIM,), 1.0, 4.0, (), jnp.float32),
        "emitted_cotangent": centred(splits[5], (TOKENS, FEATURE_DIM), 0.02, 0.119628906, ((0, 128),)),
        "paper_spans": ragged(splits[6], NDOCS, TOKENS, TOKENS // 4, 2).astype(jnp.int32),
    }


def tile_advance_update(acceptance_line_tile, lookup_line_tile, payload_line_tile, source_line_tile, reward_array, portion_number, prior_memory, evolving_memory):
    element_total, width = acceptance_line_tile.shape
    attention_heads_total, tile_length = (evolving_memory.shape[0], evolving_memory.shape[1])
    hp = lax.Precision.HIGHEST
    logw = -jnp.exp(source_line_tile)
    cum = jnp.cumsum(logw, axis=0)
    before = cum - logw
    carried = (portion_number == prior_memory).astype(jnp.float32)
    query = (acceptance_line_tile * jnp.exp(before)).reshape(element_total, attention_heads_total, tile_length)
    keyed = (lookup_line_tile * jnp.exp(-cum)).reshape(element_total, attention_heads_total, tile_length)
    values = payload_line_tile.reshape(element_total, attention_heads_total, tile_length)
    scores = jnp.einsum('jhi,shi->hjs', query, keyed, precision=hp)
    arrangement_sequence = jnp.arange(element_total)
    allowed = (arrangement_sequence[:, None] > arrangement_sequence[None, :]) & (portion_number[:, None] == portion_number[None, :])
    scores = jnp.where(allowed[None], scores, 0.0)
    concluding_answer = jnp.einsum('hjs,shc->jhc', scores, values, precision=hp)
    concluding_answer = concluding_answer + carried[:, None, None] * jnp.einsum('jhi,hic->jhc', query, evolving_memory, precision=hp)
    immediate_contribution = lax.optimization_barrier(jnp.sum((acceptance_line_tile * reward_array[None, :] * lookup_line_tile).reshape(element_total, attention_heads_total, tile_length), axis=2))
    concluding_answer = concluding_answer + immediate_contribution[:, :, None] * values
    keep = (portion_number == portion_number[-1]).astype(jnp.float32)
    ending = (lookup_line_tile * jnp.exp(cum[-1][None, :] - cum) * keep[:, None]).reshape(element_total, attention_heads_total, tile_length)
    through = jnp.exp(cum[-1]) * (portion_number[-1] == prior_memory).astype(jnp.float32)
    fresh = through.reshape(attention_heads_total, tile_length)[:, :, None] * evolving_memory + jnp.einsum('shi,shc->hic', ending, values, precision=hp)
    return (concluding_answer.reshape(element_total, width), fresh)

def reference(acceptance_gate, lookup_matrix, payload_matrix, fading_parameter, present_reward, emitted_cotangent, paper_spans):
    starts = (jnp.cumsum(paper_spans) - paper_spans).astype(jnp.int32)
    positions = jnp.arange(TOKENS, dtype=jnp.int32)
    portion_number = (lax.optimization_barrier(jnp.sum((starts[None, :] <= positions[:, None]).astype(jnp.int32), axis=1)) - 1).astype(jnp.int32)
    prevs = jnp.concatenate([jnp.full((1,), -1, jnp.int32), portion_number[:-1]]).astype(jnp.int32)
    nblocks = TOKENS // BL
    seg_blocks = portion_number.reshape(nblocks, BL)
    prev_blocks = prevs.reshape(nblocks, BL)[:, 0]

    def onward_traversal(acceptance_line_tile, lookup_line_tile, payload_line_tile, source_line_tile, reward_array):

        def step(evolving_memory, item):
            acceptance_division, lookup_division, payload_division, source_division, memory_division, location_division = item
            concluding_answer, evolving_memory = tile_advance_update(acceptance_division, lookup_division, payload_division, source_division, reward_array, memory_division, location_division, evolving_memory)
            return (evolving_memory, concluding_answer)
        items = (acceptance_line_tile.reshape(nblocks, BL, FEATURE_DIM), lookup_line_tile.reshape(nblocks, BL, FEATURE_DIM), payload_line_tile.reshape(nblocks, BL, FEATURE_DIM), source_line_tile.reshape(nblocks, BL, FEATURE_DIM), seg_blocks, prev_blocks)
        start = jnp.zeros((HEADS, HS, HS), jnp.float32)
        spare_placeholder, results = lax.scan(jax.checkpoint(step), start, items)
        return results.reshape(TOKENS, FEATURE_DIM)
    spare_placeholder, adjoint_mapping = jax.vjp(onward_traversal, acceptance_gate.astype(jnp.float32), lookup_matrix.astype(jnp.float32), payload_matrix.astype(jnp.float32), fading_parameter, present_reward)
    derivative_bundle = adjoint_mapping(emitted_cotangent.astype(jnp.float32))
    return (derivative_bundle[0].astype(jnp.bfloat16), derivative_bundle[1].astype(jnp.bfloat16), derivative_bundle[2].astype(jnp.bfloat16), derivative_bundle[3].astype(jnp.bfloat16), derivative_bundle[4])
```

```python
import jax
import jax.numpy as jnp
from jax import lax
from jax.experimental import pallas as pl
from jax.experimental.pallas import tpu as pltpu
from jax.sharding import PartitionSpec as P

HS = 64
LANES = 128
TOK = 128
STATE_ROWS = 8
ROWS = 24
PAIRS = 4
F32 = jnp.float32
BF16 = jnp.bfloat16

NN = (((1,), (0,)), ((), ()))
NT = (((1,), (1,)), ((), ()))
TN = (((0,), (0,)), ((), ()))


def dot(a, b, dims):
    return lax.dot_general(a, b, dims, preferred_element_type=F32)


def halves(x):
    high = x.astype(BF16)
    return high, (x - high.astype(F32)).astype(BF16)


def head_masks():
    lane = lax.broadcasted_iota(jnp.int32, (1, LANES), 1)
    return (lane < HS).astype(F32).astype(BF16), (lane >= HS).astype(F32).astype(BF16)


def by_head(x, masks):
    return jnp.concatenate([x * masks[0], x * masks[1]], axis=0)


def side_by_side(x):
    return jnp.concatenate([x[:TOK], x[TOK:]], axis=1)


def cat(*parts, axis):
    return jnp.concatenate(parts, axis=axis)


def square(n=TOK):
    row = lax.broadcasted_iota(jnp.int32, (n, n), 0)
    return row, lax.broadcasted_iota(jnp.int32, (n, n), 1)


def ones_by_head():
    row, col = square()
    same = ((row < HS) == (col < HS)).astype(F32).astype(BF16)
    return cat(same, same, axis=0)


def head_sums(x, ones):
    high, low = halves(x)
    return dot(cat(high, low, axis=1), ones, NN)


def segments(spans, base):
    ndocs = spans.shape[1]
    row, col = square(ndocs)
    ends_down = jnp.sum(jnp.where(col <= row, spans, 0.0), axis=1, keepdims=True)
    spans_down = jnp.sum(jnp.where(col == row, spans, 0.0), axis=1, keepdims=True)
    ends = jnp.sum(jnp.where(row <= col, spans_down, 0.0), axis=0, keepdims=True)
    across = (base + lax.broadcasted_iota(jnp.int32, (1, TOK), 1)).astype(F32)
    down = (base + lax.broadcasted_iota(jnp.int32, (TOK, 1), 0)).astype(F32)
    seg_across = jnp.sum(jnp.where(ends_down <= across, 1.0, 0.0), axis=0, keepdims=True)
    seg_down = jnp.sum(jnp.where(ends <= down, 1.0, 0.0), axis=1, keepdims=True)
    prev = jnp.sum(jnp.where(ends <= down[:1] - 1.0, 1.0, 0.0), axis=1, keepdims=True)
    return seg_across, seg_down, jnp.where(down[:1] > 0.0, prev, -1.0)


def summary_kernel(rank, spans, r, k, v, g, x, out, cum_out, masks_out, keep, carried, passes):
    @pl.when(pl.program_id(0) == 0)
    def _():
        seg_across, seg_down, prev = segments(spans[...].astype(F32), rank[0] * TOK)
        row, col = square()
        same = seg_down == seg_across
        last = seg_down[TOK - 1 :]
        keep[...] = jnp.broadcast_to((seg_down == last).astype(F32), (TOK, LANES))
        carried[...] = jnp.broadcast_to((seg_down == prev).astype(F32), (TOK, LANES))
        passes[...] = jnp.broadcast_to((last == prev).astype(F32), passes.shape)
        masks_out[0] = (same & (row > col)).astype(F32)
        masks_out[1] = (same & (row < col)).astype(F32)
        masks_out[2] = keep[...]
        masks_out[3] = carried[...]

    row, col = square()
    lower = (row >= col).astype(F32).astype(BF16)
    lower = cat(lower, lower, axis=1)
    ones = ones_by_head()
    lane = lax.broadcasted_iota(jnp.int32, (HS, LANES), 1)
    for pair in range(PAIRS):
        at = slice(pair * LANES, (pair + 1) * LANES)
        logw = -jnp.exp(x[:, at])
        cum = dot(lower, cat(*halves(logw), axis=0), NN)
        cum_out[:, at] = cum
        last = cum[TOK - 1 :]
        rp, kp = r[:, at].astype(F32), k[:, at].astype(F32)
        ending = cat(*halves(kp * jnp.exp(last - cum) * keep[...]), axis=1)
        reached = cat(*halves(rp * jnp.exp(cum - logw) * carried[...]), axis=1)
        ends, pulls = dot(v[:, at], ending, TN), dot(g[:, at], reached, TN)
        bonus = head_sums(g[:, at].astype(F32) * v[:, at].astype(F32), ones)
        bonus = jnp.sum(rp * kp * bonus, axis=0, keepdims=True)
        through = jnp.exp(last) * passes[:1]
        peers = slice(pair * STATE_ROWS, (pair + 1) * STATE_ROWS)
        for place, both in ((0, ends), (1, pulls)):
            both = both[:, :LANES] + both[:, LANES:]
            state = jnp.where(lane < HS, both[:HS], both[HS:])
            out[peers, place * STATE_ROWS : (place + 1) * STATE_ROWS] = state.reshape(
                HS // STATE_ROWS, STATE_ROWS, LANES
            )
        rest = cat(through, bonus, jnp.zeros((6, LANES), F32), axis=0)
        out[peers, 2 * STATE_ROWS :] = jnp.broadcast_to(rest[None], (STATE_ROWS, 8, LANES))


def scan_kernel(got, out):
    shards = got.shape[0]
    state = jnp.zeros((STATE_ROWS, LANES), F32)
    bonus = jnp.zeros((8, LANES), F32)
    for at in range(shards):
        out[at, :STATE_ROWS] = state
        rest = got[at, 2 * STATE_ROWS :]
        state = rest[:1] * state + got[at, :STATE_ROWS]
        bonus = bonus + rest
    state = jnp.zeros((STATE_ROWS, LANES), F32)
    for at in reversed(range(shards)):
        out[at, STATE_ROWS : 2 * STATE_ROWS] = state
        state = got[at, 2 * STATE_ROWS : 2 * STATE_ROWS + 1] * state + got[at, STATE_ROWS : 2 * STATE_ROWS]
        out[at, 2 * STATE_ROWS :] = bonus


def inside_kernel(r, k, v, g, x, cum_in, u, masks, dr, dk, dv, dl):
    heads = head_masks()
    ones = ones_by_head()
    row, col = square()
    after = (row < col).astype(F32).astype(BF16)
    onward = -((row <= col).astype(F32).astype(BF16))
    sums = cat(after, onward, axis=1)
    allowed = cat(masks[0], masks[0], axis=0)
    allowed_t = cat(masks[1], masks[1], axis=0)
    for pair in range(PAIRS):
        at = slice(pair * LANES, (pair + 1) * LANES)
        rb, kb, vb, gb = r[:, at], k[:, at], v[:, at], g[:, at]
        rp, kp, vp, gp = (part.astype(F32) for part in (rb, kb, vb, gb))
        cum = cum_in[:, at]
        middle = 0.5 * cum[TOK - 1 :]
        scale_r = jnp.exp(cum + jnp.exp(x[:, at]) - middle)
        scale_k = jnp.exp(middle - cum)
        rh, rl = halves(rp * scale_r)
        kh, kl = halves(kp * scale_k)
        rh2, rl2, kh2, kl2 = (by_head(part, heads) for part in (rh, rl, kh, kl))
        g2, v2 = by_head(gb, heads), by_head(vb, heads)
        scores = dot(cat(kh2, kl2, axis=1), cat(rh, rh, axis=1), NT) + dot(kh2, rl, NT)
        scores = jnp.where(allowed_t > 0.0, scores, 0.0)
        sh, sl = halves(side_by_side(scores))
        direct = u[:, at]
        dv[:, at] = dot(sh, g2, NN) + dot(sl, g2, NN) + head_sums(rp * direct * kp, ones) * gp
        pull = side_by_side(dot(g2, vb, NT) * allowed)
        pull_t = side_by_side(dot(v2, gb, NT) * allowed_t)
        ph, plow = halves(pull)
        th, tl = halves(pull_t)
        dri = scale_r * (dot(ph, kh2, NN) + dot(ph, kl2, NN) + dot(plow, kh2, NN))
        dki = scale_k * (dot(th, rh2, NN) + dot(th, rl2, NN) + dot(tl, rh2, NN))
        own = direct * head_sums(gp * vp, ones)
        dr[:, at] = dri + own * kp
        dk[:, at] = dki + own * rp
        high, low = halves(cat(rp * dri, kp * dki, axis=0))
        dl[:, at] = dot(sums, high, NN) + dot(sums, low, NN)


def final_kernel(r, k, v, g, x, cum_in, masks, dri, dki, dvi, dli, got, dr, dk, dv, dx, du):
    heads = head_masks()
    row, col = square()
    after = (row < col).astype(F32).astype(BF16)
    earlier = (row > col).astype(F32).astype(BF16)
    sums = cat(after, earlier, axis=1)
    for pair in range(PAIRS):
        at = slice(pair * LANES, (pair + 1) * LANES)
        peers = slice(pair * STATE_ROWS, (pair + 1) * STATE_ROWS)
        state = got[peers, :STATE_ROWS].reshape(HS, LANES)
        dstate = got[peers, STATE_ROWS : 2 * STATE_ROWS].reshape(HS, LANES)
        du[:, at] = got[pair * STATE_ROWS, 2 * STATE_ROWS + 1 : 2 * STATE_ROWS + 2]
        rp, kp = r[:, at].astype(F32), k[:, at].astype(F32)
        cum = cum_in[:, at]
        last = cum[TOK - 1 :]
        rate = jnp.exp(x[:, at])
        kd = jnp.exp(last - cum) * masks[2]
        rd = jnp.exp(cum + rate) * masks[3]
        sh, sl = (by_head(part, heads) for part in halves(state))
        dh, dlow = (by_head(part, heads) for part in halves(dstate))
        drs = rd * (dot(g[:, at], sh, NN) + dot(g[:, at], sl, NN))
        dks = kd * (dot(v[:, at], dh, NN) + dot(v[:, at], dlow, NN))
        eh, el = halves(kp * kd)
        dvs = dot(eh, dh, NT) + dot(eh, dlow, NT) + dot(el, dh, NT)
        dr[:, at] = (dri[:, at] + drs).astype(BF16)
        dk[:, at] = (dki[:, at] + dks).astype(BF16)
        dv[:, at] = (dvi[:, at] + dvs).astype(BF16)
        high, low = halves(cat(rp * drs, kp * dks, axis=0))
        both = masks[2][TOK - 1 :] * masks[3][TOK - 1 :]
        across = jnp.exp(last) * both * jnp.sum(state * dstate, axis=0, keepdims=True)
        grad = dli[:, at] + dot(sums, high, NN) + dot(sums, low, NN) + across
        dx[:, at] = (-rate * grad).astype(BF16)


def body(r, k, v, x, u, g, spans):
    tokens, width = r.shape
    npairs = width // LANES
    peers = lax.axis_size("seq")
    steps = npairs // PAIRS
    part = PAIRS * LANES
    rank = lax.axis_index("seq").astype(jnp.int32).reshape(1)
    wide = pl.BlockSpec((TOK, part), lambda i, *_: (0, i))
    thin = pl.BlockSpec((1, part), lambda i, *_: (0, i))
    sent = pl.BlockSpec((PAIRS * STATE_ROWS, ROWS, LANES), lambda i, *_: (i, 0, 0))
    fixed = pl.BlockSpec((4, TOK, LANES), lambda i, *_: (0, 0, 0))
    full = jax.ShapeDtypeStruct((tokens, width), F32)
    rounded = jax.ShapeDtypeStruct((tokens, width), BF16)
    packet = jax.ShapeDtypeStruct((peers, ROWS, LANES), F32)

    summaries, cum, masks = pl.pallas_call(
        summary_kernel,
        grid_spec=pltpu.PrefetchScalarGridSpec(
            num_scalar_prefetch=1,
            grid=(steps,),
            in_specs=[pl.BlockSpec((1, spans.shape[0]), lambda i, *_: (0, 0))] + [wide] * 5,
            out_specs=[sent, wide, fixed],
            scratch_shapes=[
                pltpu.VMEM((TOK, LANES), F32),
                pltpu.VMEM((TOK, LANES), F32),
                pltpu.VMEM((8, LANES), F32),
            ],
        ),
        out_shape=[packet, full, jax.ShapeDtypeStruct((4, TOK, LANES), F32)],
        name="summary",
        cost_estimate=pl.CostEstimate(flops=10**9, bytes_accessed=6 * 10**6, transcendentals=10**6),
    )(rank, spans.reshape(1, -1), r, k, v, g, x)
    got = lax.all_to_all(summaries, "seq", 0, 0, tiled=True)
    dri, dki, dvi, dli = pl.pallas_call(
        inside_kernel,
        grid=(steps,),
        in_specs=[wide] * 6 + [thin, fixed],
        out_specs=[wide] * 4,
        out_shape=[full] * 4,
        name="inside",
        cost_estimate=pl.CostEstimate(flops=10**10, bytes_accessed=10**7, transcendentals=10**6),
    )(r, k, v, g, x, cum, u.reshape(1, -1), masks)
    states = pl.pallas_call(
        scan_kernel,
        out_shape=packet,
        name="scan",
        cost_estimate=pl.CostEstimate(flops=10**6, bytes_accessed=3 * 10**6, transcendentals=0),
    )(got)
    returned = lax.all_to_all(states, "seq", 0, 0, tiled=True)
    dr, dk, dv, dx, du = pl.pallas_call(
        final_kernel,
        grid=(steps,),
        in_specs=[wide] * 6 + [fixed] + [wide] * 4 + [sent],
        out_specs=[wide] * 4 + [thin],
        out_shape=[rounded] * 4 + [jax.ShapeDtypeStruct((1, width), F32)],
        name="final",
        cost_estimate=pl.CostEstimate(flops=10**9, bytes_accessed=10**7, transcendentals=10**6),
    )(r, k, v, g, x, cum, masks, dri, dki, dvi, dli, returned)
    return dr, dk, dv, dx, du.reshape(width)


def solution(mesh):
    split, whole = P("seq", None), P()
    return jax.shard_map(
        body,
        mesh=mesh,
        in_specs=(split, split, split, split, whole, split, whole),
        out_specs=(split, split, split, split, whole),
        check_vma=False,
    )
```

```python
import jax
import jax.numpy as jnp
from jax import lax
from jax.experimental import pallas as pl
from jax.experimental.pallas import tpu as pltpu
from jax.sharding import PartitionSpec as P

HS = 64
LANES = 128
TOK = 128
BLOCKS = 8
STATE_ROWS = HS // BLOCKS
ROWS_OUT = 18
ROWS_BACK = 17
PAIRS = 8
VMEM = 24 * 2**20
WRITE = 4
F32 = jnp.float32
BF16 = jnp.bfloat16

FULL_ROWS = [slice(n * TOK, (n + 1) * TOK) for n in range(9)]
FULL_TOK = 9 * TOK
HALF_ROWS = [slice(n * TOK, (n + 1) * TOK) for n in range(3)]

NN = (((1,), (0,)), ((), ()))
NT = (((1,), (1,)), ((), ()))
TN = (((0,), (0,)), ((), ()))


def dot(a, b, dims):
    return lax.dot_general(a, b, dims, preferred_element_type=F32)


def halves(x):
    high = x.astype(BF16)
    return high, (x - high.astype(F32)).astype(BF16)


def head_masks():
    lane = lax.broadcasted_iota(jnp.int32, (1, LANES), 1)
    return (lane < HS).astype(F32).astype(BF16), (lane >= HS).astype(F32).astype(BF16)


def by_head(x, masks):
    return jnp.concatenate([x * masks[0], x * masks[1]], axis=0)


def side_by_side(x):
    return jnp.concatenate([x[:TOK], x[TOK:]], axis=1)


def cat(*parts, axis):
    return jnp.concatenate(parts, axis=axis)


def square(n=TOK):
    row = lax.broadcasted_iota(jnp.int32, (n, n), 0)
    return row, lax.broadcasted_iota(jnp.int32, (n, n), 1)


def ones_by_head():
    row, col = square()
    same = ((row < HS) == (col < HS)).astype(F32).astype(BF16)
    return cat(same, same, axis=0)


def head_sums(x, ones):
    high, low = halves(x)
    return dot(cat(high, low, axis=1), ones, NN)


def segments(spans, base):
    ndocs = spans.shape[1]
    row, col = square(ndocs)
    ends_down = jnp.sum(jnp.where(col <= row, spans, 0.0), axis=1, keepdims=True)
    spans_down = jnp.sum(jnp.where(col == row, spans, 0.0), axis=1, keepdims=True)
    ends = jnp.sum(jnp.where(row <= col, spans_down, 0.0), axis=0, keepdims=True)
    across = (base + lax.broadcasted_iota(jnp.int32, (1, TOK), 1)).astype(F32)
    down = (base + lax.broadcasted_iota(jnp.int32, (TOK, 1), 0)).astype(F32)
    seg_across = jnp.sum(jnp.where(ends_down <= across, 1.0, 0.0), axis=0, keepdims=True)
    seg_down = jnp.sum(jnp.where(ends <= down, 1.0, 0.0), axis=1, keepdims=True)
    prev = jnp.sum(jnp.where(ends <= down[:1] - 1.0, 1.0, 0.0), axis=1, keepdims=True)
    return seg_across, seg_down, jnp.where(down[:1] > 0.0, prev, -1.0)


def summary_kernel(rank, spans, r, k, v, g, x, out, cum_out, masks_out, keep, carried, passes):
    @pl.when(pl.program_id(0) == 0)
    def _():
        seg_across, seg_down, prev = segments(spans[...].astype(F32), rank[0] * TOK)
        row, col = square()
        same = seg_down == seg_across
        last = seg_down[TOK - 1 :]
        keep[...] = jnp.broadcast_to((seg_down == last).astype(F32), (TOK, LANES))
        carried[...] = jnp.broadcast_to((seg_down == prev).astype(F32), (TOK, LANES))
        passes[...] = jnp.broadcast_to((last == prev).astype(F32), passes.shape)
        masks_out[0] = (same & (row > col)).astype(F32)
        masks_out[1] = (same & (row < col)).astype(F32)
        masks_out[2] = keep[...]
        masks_out[3] = carried[...]

    row, col = square()
    lower = (row >= col).astype(F32).astype(BF16)
    lower = cat(lower, lower, axis=1)
    ones = ones_by_head()
    lane = lax.broadcasted_iota(jnp.int32, (HS, LANES), 1)
    for pair in range(PAIRS):
        at = slice(pair * LANES, (pair + 1) * LANES)
        logw = -jnp.exp(x[:, at])
        cum = dot(lower, cat(*halves(logw), axis=0), NN)
        cum_out[:, at] = cum
        last = cum[TOK - 1 :]
        rp, kp = r[:, at].astype(F32), k[:, at].astype(F32)
        ending = cat(*halves(kp * jnp.exp(last - cum) * keep[...]), axis=1)
        reached = cat(*halves(rp * jnp.exp(cum - logw) * carried[...]), axis=1)
        ends, pulls = dot(v[:, at], ending, TN), dot(g[:, at], reached, TN)
        bonus = head_sums(g[:, at].astype(F32) * v[:, at].astype(F32), ones)
        bonus = jnp.sum(rp * kp * bonus, axis=0, keepdims=True)
        through = jnp.exp(last) * passes[:1]
        rest = cat(through, bonus, axis=0)
        states = []
        for both in (ends, pulls):
            both = both[:, :LANES] + both[:, LANES:]
            states.append(jnp.where(lane < HS, both[:HS], both[HS:]))
        for peer in range(BLOCKS):
            at = (pair * BLOCKS + peer) * ROWS_OUT
            for place, state in enumerate(states):
                row = at + place * STATE_ROWS
                out[row : row + STATE_ROWS] = state[peer * STATE_ROWS : (peer + 1) * STATE_ROWS]
            out[at + 2 * STATE_ROWS : at + ROWS_OUT] = rest


def scan_kernel(got, done, out):
    del done
    shards = got.shape[0] // ROWS_OUT
    state = jnp.zeros((STATE_ROWS, LANES), F32)
    bonus = jnp.zeros((1, LANES), F32)
    for shard in range(shards):
        at, to = shard * ROWS_OUT, shard * ROWS_BACK
        out[to : to + STATE_ROWS] = state
        through = got[at + 2 * STATE_ROWS : at + 2 * STATE_ROWS + 1]
        state = through * state + got[at : at + STATE_ROWS]
        bonus = bonus + got[at + 2 * STATE_ROWS + 1 : at + ROWS_OUT]
    state = jnp.zeros((STATE_ROWS, LANES), F32)
    for shard in reversed(range(shards)):
        at, to = shard * ROWS_OUT, shard * ROWS_BACK
        out[to + STATE_ROWS : to + 2 * STATE_ROWS] = state
        out[to + 2 * STATE_ROWS : to + ROWS_BACK] = bonus
        through = got[at + 2 * STATE_ROWS : at + 2 * STATE_ROWS + 1]
        state = through * state + got[at + STATE_ROWS : at + 2 * STATE_ROWS]


def inside_kernel(r, k, v, g, x, cum_in, u, masks, full_out, half_out, done):
    done[...] = jnp.zeros(done.shape, F32)
    dr, dk, dv, dl, rd, kd, pr, pk, rate = (full_out.at[rows] for rows in FULL_ROWS)
    el, gc, vc = (half_out.at[rows] for rows in HALF_ROWS)
    through = full_out.at[FULL_TOK:]
    heads = head_masks()
    ones = ones_by_head()
    row, col = square()
    after = (row < col).astype(F32).astype(BF16)
    onward = -((row <= col).astype(F32).astype(BF16))
    sums = cat(after, onward, axis=1)
    allowed = cat(masks[0], masks[0], axis=0)
    allowed_t = cat(masks[1], masks[1], axis=0)
    both = masks[2][TOK - 1 :] * masks[3][TOK - 1 :]
    for pair in range(PAIRS):
        at = slice(pair * LANES, (pair + 1) * LANES)
        rb, kb, vb, gb = r[:, at], k[:, at], v[:, at], g[:, at]
        rp, kp, vp, gp = (part.astype(F32) for part in (rb, kb, vb, gb))
        cum = cum_in[:, at]
        last = cum[TOK - 1 :]
        middle = 0.5 * last
        speed = jnp.exp(x[:, at])
        scale_r = jnp.exp(cum + speed - middle)
        scale_k = jnp.exp(middle - cum)
        rh, rl = halves(rp * scale_r)
        kh, kl = halves(kp * scale_k)
        rh2, rl2, kh2, kl2 = (by_head(part, heads) for part in (rh, rl, kh, kl))
        g2, v2 = by_head(gb, heads), by_head(vb, heads)
        scores = dot(cat(kh2, kl2, axis=1), cat(rh, rh, axis=1), NT) + dot(kh2, rl, NT)
        scores = jnp.where(allowed_t > 0.0, scores, 0.0)
        sh, sl = halves(side_by_side(scores))
        direct = u[:, at]
        dv[:, at] = dot(sh, g2, NN) + dot(sl, g2, NN) + head_sums(rp * direct * kp, ones) * gp
        pull = side_by_side(dot(g2, vb, NT) * allowed)
        pull_t = side_by_side(dot(v2, gb, NT) * allowed_t)
        ph, plow = halves(pull)
        th, tl = halves(pull_t)
        dri = scale_r * (dot(ph, kh2, NN) + dot(ph, kl2, NN) + dot(plow, kh2, NN))
        dki = scale_k * (dot(th, rh2, NN) + dot(th, rl2, NN) + dot(tl, rh2, NN))
        own = direct * head_sums(gp * vp, ones)
        dr[:, at] = dri + own * kp
        dk[:, at] = dki + own * rp
        high, low = halves(cat(rp * dri, kp * dki, axis=0))
        dl[:, at] = dot(sums, high, NN) + dot(sums, low, NN)
        reached = jnp.exp(cum + speed) * masks[3]
        kept = jnp.exp(last - cum) * masks[2]
        rd[:, at] = reached
        kd[:, at] = kept
        pr[:, at] = rp * reached
        ending = kp * kept
        pk[:, at] = ending
        high, low = halves(ending)
        el[:, at] = low
        rate[:, at] = speed
        through[:, at] = jnp.broadcast_to(jnp.exp(last) * both, (8, LANES))
        gc[:, at] = gb
        vc[:, at] = vb


def final_kernel(full, half, got, dr, dk, dv, dx, du, rounded, sems):
    heads = head_masks()
    row, col = square()
    after = (row < col).astype(F32).astype(BF16)
    earlier = (row > col).astype(F32).astype(BF16)
    sums = cat(after, earlier, axis=1)
    dri, dki, dvi, dli, rd, kd, pr, pk, rate = (full.at[rows] for rows in FULL_ROWS)
    el_in, g, v = (half.at[rows] for rows in HALF_ROWS)
    copies = []
    for pair in range(du.shape[1] // LANES):
        at = slice(pair * LANES, (pair + 1) * LANES)
        rows = [(pair * BLOCKS + peer) * ROWS_BACK for peer in range(BLOCKS)]
        state = cat(*(got[row : row + STATE_ROWS] for row in rows), axis=0)
        dstate = cat(*(got[row + STATE_ROWS : row + 2 * STATE_ROWS] for row in rows), axis=0)
        du[:, at] = got[rows[0] + 2 * STATE_ROWS : rows[0] + ROWS_BACK]
        sh, sl = (by_head(part, heads) for part in halves(state))
        dh, dlow = (by_head(part, heads) for part in halves(dstate))
        gb, vb = g[:, at], v[:, at]
        reach = dot(cat(gb, gb, axis=1), cat(sh, sl, axis=0), NN)
        pull = dot(cat(vb, vb, axis=1), cat(dh, dlow, axis=0), NN)
        ending = pk[:, at]
        eh, el = ending.astype(BF16), el_in[:, at]
        dvs = dot(cat(eh, el, axis=1), cat(dh, dh, axis=1), NT) + dot(eh, dlow, NT)
        rounded[0, :, at] = (dri[:, at] + rd[:, at] * reach).astype(BF16)
        rounded[1, :, at] = (dki[:, at] + kd[:, at] * pull).astype(BF16)
        rounded[2, :, at] = (dvi[:, at] + dvs).astype(BF16)
        moved = dot(sums, cat(*halves(cat(pr[:, at] * reach, ending * pull, axis=0)), axis=1), NN)
        across = full[FULL_TOK : FULL_TOK + 1, at] * jnp.sum(state * dstate, axis=0, keepdims=True)
        grad = dli[:, at] + moved[:, :LANES] + moved[:, LANES:] + across
        rounded[3, :, at] = (-rate[:, at] * grad).astype(BF16)
        if (pair + 1) % WRITE == 0:
            ready = slice((pair + 1 - WRITE) * LANES, (pair + 1) * LANES)
            for n, out in enumerate((dr, dk, dv, dx)):
                sem = sems.at[pair // WRITE, n]
                copies.append(pltpu.make_async_copy(rounded.at[n, :, ready], out.at[:, ready], sem))
                copies[-1].start()
    for copy in copies:
        copy.wait()


def hbm(x):
    return pltpu.with_memory_space_constraint(x, pltpu.HBM)


def vm(x):
    return pltpu.with_memory_space_constraint(x, pltpu.VMEM)


def exchange(rows, peers):
    packets = rows.reshape(peers, -1, 1, LANES)
    return lax.all_to_all(packets, "seq", 0, 0, tiled=True).reshape(rows.shape)


def body(r, k, v, x, u, g, spans):
    tokens, width = r.shape
    npairs = width // LANES
    peers = lax.axis_size("seq")
    steps = npairs // PAIRS
    part = PAIRS * LANES
    r, k, v, x, g, u = (hbm(part) for part in (r, k, v, x, g, u.reshape(1, -1)))
    rank = lax.axis_index("seq").astype(jnp.int32).reshape(1)
    wide = pl.BlockSpec((TOK, part), lambda i, *_: (0, i))
    thin = pl.BlockSpec((1, part), lambda i, *_: (0, i))
    sent = pl.BlockSpec((PAIRS * BLOCKS * ROWS_OUT, LANES), lambda i, *_: (i, 0))
    whole = pl.BlockSpec(memory_space=pltpu.VMEM)
    fixed = pl.BlockSpec((4, TOK, LANES), lambda i, *_: (0, 0, 0))

    summaries, cum, masks = pl.pallas_call(
        summary_kernel,
        grid_spec=pltpu.PrefetchScalarGridSpec(
            num_scalar_prefetch=1,
            grid=(steps,),
            in_specs=[pl.BlockSpec((1, spans.shape[0]), lambda i, *_: (0, 0))] + [wide] * 5,
            out_specs=[sent, wide, fixed],
            scratch_shapes=[
                pltpu.VMEM((TOK, LANES), F32),
                pltpu.VMEM((TOK, LANES), F32),
                pltpu.VMEM((8, LANES), F32),
            ],
        ),
        out_shape=[
            pltpu.HBM((peers * ROWS_OUT, LANES), F32),
            pltpu.HBM((tokens, width), F32),
            pltpu.HBM((4, TOK, LANES), F32),
        ],
        name="summary",
        compiler_params=pltpu.CompilerParams(vmem_limit_bytes=VMEM),
        cost_estimate=pl.CostEstimate(flops=10**9, bytes_accessed=6 * 10**6, transcendentals=10**6),
    )(rank, hbm(spans.reshape(1, -1)), r, k, v, g, x)
    got = exchange(summaries, peers)
    full, half, done = pl.pallas_call(
        inside_kernel,
        grid=(steps,),
        in_specs=[wide] * 6 + [thin, fixed],
        out_specs=[
            pl.BlockSpec((FULL_TOK + 8, part), lambda i, *_: (0, i)),
            pl.BlockSpec((3 * TOK, part), lambda i, *_: (0, i)),
            pl.BlockSpec((8, LANES), lambda i, *_: (0, 0)),
        ],
        out_shape=[
            pltpu.HBM((FULL_TOK + 8, width), F32),
            pltpu.HBM((3 * TOK, width), BF16),
            pltpu.HBM((8, LANES), F32),
        ],
        name="inside",
        compiler_params=pltpu.CompilerParams(vmem_limit_bytes=VMEM),
        cost_estimate=pl.CostEstimate(flops=10**10, bytes_accessed=10**7, transcendentals=10**6),
    )(r, k, v, g, x, hbm(cum), u, hbm(masks))
    states = pl.pallas_call(
        scan_kernel,
        in_specs=[whole, pl.BlockSpec(memory_space=pl.ANY)],
        out_shape=pltpu.VMEM((peers * ROWS_BACK, LANES), F32),
        name="scan",
        compiler_params=pltpu.CompilerParams(vmem_limit_bytes=VMEM),
        cost_estimate=pl.CostEstimate(flops=10**10, bytes_accessed=3 * 10**7, transcendentals=0),
    )(vm(got), hbm(done))
    returned = exchange(states, peers)
    dr, dk, dv, dx, du = pl.pallas_call(
        final_kernel,
        in_specs=[whole] * 3,
        out_specs=[pl.BlockSpec(memory_space=pl.ANY)] * 4 + [whole],
        out_shape=[pltpu.HBM((tokens, width), BF16)] * 4 + [jax.ShapeDtypeStruct((1, width), F32)],
        scratch_shapes=[
            pltpu.VMEM((4, tokens, width), BF16),
            pltpu.SemaphoreType.DMA((npairs // WRITE, 4)),
        ],
        name="final",
        compiler_params=pltpu.CompilerParams(vmem_limit_bytes=VMEM),
        cost_estimate=pl.CostEstimate(flops=10**9, bytes_accessed=10**7, transcendentals=10**6),
    )(vm(full), vm(half), vm(returned))
    return dr, dk, dv, dx, du.reshape(width)


def solution(mesh):
    split, whole = P("seq", None), P()
    return jax.shard_map(
        body,
        mesh=mesh,
        in_specs=(split, split, split, split, whole, split, whole),
        out_specs=(split, split, split, split, whole),
        check_vma=False,
    )
```

```python
import jax
import jax.numpy as jnp
from jax import lax
from jax.experimental import pallas as pl
from jax.experimental.pallas import tpu as pltpu
from jax.sharding import Mesh
from jax.sharding import PartitionSpec as P

HS = 64
LANES = 128
TOK = 128
CORES = 2
HALF = 8
BLOCKS = 8
STATE_ROWS = HS // BLOCKS
ROWS_OUT = 18
ROWS_BACK = 17
PULL = HALF * HS
DECAY = 2 * PULL
BONUS = DECAY + HALF
GROUP = 4
INSIDE = 4
PAIRS = 8
VMEM = 24 * 2**20
WRITE = 4
LOG2_E = 1.4426950408889634
LOG2_LOG2_E = 0.5287663729448977
LN_2 = 0.6931471805599453
F32 = jnp.float32
BF16 = jnp.bfloat16

FULL_ROWS = [slice(n * TOK, (n + 1) * TOK) for n in range(9)]
FULL_TOK = 9 * TOK
HALF_ROWS = [slice(n * TOK, (n + 1) * TOK) for n in range(3)]

NN = (((1,), (0,)), ((), ()))
NT = (((1,), (1,)), ((), ()))
TN = (((0,), (0,)), ((), ()))


def dot(a, b, dims):
    return lax.dot_general(a, b, dims, preferred_element_type=F32)


def halves(x):
    high = x.astype(BF16)
    return high, (x - high.astype(F32)).astype(BF16)


def head_masks():
    lane = lax.broadcasted_iota(jnp.int32, (1, LANES), 1)
    return (lane < HS).astype(F32).astype(BF16), (lane >= HS).astype(F32).astype(BF16)


def by_head(x, masks):
    return jnp.concatenate([x * masks[0], x * masks[1]], axis=0)


def side_by_side(x):
    return jnp.concatenate([x[:TOK], x[TOK:]], axis=1)


def cat(*parts, axis):
    return jnp.concatenate(parts, axis=axis)


def square(n=TOK):
    row = lax.broadcasted_iota(jnp.int32, (n, n), 0)
    return row, lax.broadcasted_iota(jnp.int32, (n, n), 1)


def ones_by_head():
    row, col = square()
    same = ((row < HS) == (col < HS)).astype(F32).astype(BF16)
    return cat(same, same, axis=0)


def head_sums(x, ones):
    high, low = halves(x)
    return dot(cat(high, low, axis=1), ones, NN)


def segments(spans, base):
    ndocs = spans.shape[1]
    row, col = square(ndocs)
    upper = (row <= col).astype(F32).astype(BF16)
    spans = jnp.broadcast_to(spans, (8, ndocs))
    coarse, fine = ((part.astype(F32)).astype(BF16) for part in (spans >> 6, spans & 63))
    ends = (64.0 * dot(coarse, upper, NN) + dot(fine, upper, NN))[:1]
    down = (base + lax.broadcasted_iota(jnp.int32, (TOK, 1), 0)).astype(F32)
    seg_down = jnp.sum(jnp.where(ends <= down, 1.0, 0.0), axis=1, keepdims=True)
    row, col = square()
    seg_across = jnp.sum(jnp.where(row == col, seg_down, 0.0), axis=0, keepdims=True)
    prev = jnp.sum(jnp.where(ends <= down[:1] - 1.0, 1.0, 0.0), axis=1, keepdims=True)
    return seg_across, seg_down, jnp.where(down[:1] > 0.0, prev, -1.0)


def decay_rate(x):
    return jnp.exp2(x * LOG2_E + LOG2_LOG2_E)


def summary_kernel(spans, r, k, v, g, x, out, cum_out, masks_out, keep, carried, passes):
    @pl.when(pl.program_id(0) == 0)
    def _():
        seg_across, seg_down, prev = segments(spans[...], (lax.axis_index("chip") * CORES + lax.axis_index("core")) * TOK)
        row, col = square()
        same = seg_down == seg_across
        last = seg_down[TOK - 1 :]
        keep[...] = jnp.broadcast_to((seg_down == last).astype(F32), (TOK, LANES))
        carried[...] = jnp.broadcast_to((seg_down == prev).astype(F32), (TOK, LANES))
        passes[...] = jnp.broadcast_to((last == prev).astype(F32), passes.shape)
        masks_out[0] = (same & (row > col)).astype(F32)
        masks_out[1] = (same & (row < col)).astype(F32)
        masks_out[2] = keep[...]
        masks_out[3] = carried[...]

    row, col = square()
    lower = (row >= col).astype(F32).astype(BF16)
    lower = cat(lower, lower, axis=1)
    ones = ones_by_head()
    lane = lax.broadcasted_iota(jnp.int32, (HS, LANES), 1)
    spots = [slice(pair * LANES, (pair + 1) * LANES) for pair in range(PAIRS)]
    for group in range(0, PAIRS, GROUP):
        wide = slice(group * LANES, (group + GROUP) * LANES)
        cum_out[:, wide] = dot(lower, cat(*halves(decay_rate(x[:, wide])), axis=0), NN)
    products = [cat(*halves(g[:, at].astype(F32) * v[:, at].astype(F32)), axis=1) for at in spots]
    bonuses = dot(cat(*products, axis=0), ones, NN)
    endings, reaches = [], []
    for at in spots:
        cum = cum_out[:, at]
        rp, kp = r[:, at].astype(F32), k[:, at].astype(F32)
        ending = kp * jnp.exp2(cum - cum[TOK - 1 :]) * keep[...]
        reached = rp * jnp.exp2(decay_rate(x[:, at]) - cum) * carried[...]
        endings.append(cat(*halves(ending), axis=1))
        reaches.append(cat(*halves(reached), axis=1))
    ends = [dot(v[:, at], ending, TN) for at, ending in zip(spots, endings)]
    pulls = [dot(g[:, at], reached, TN) for at, reached in zip(spots, reaches)]
    for pair, at in enumerate(spots):
        for place, both in ((0, ends[pair]), (PULL, pulls[pair])):
            both = both[:, :LANES] + both[:, LANES:]
            state = jnp.where(lane < HS, both[:HS], both[HS:])
            out[0, place + pair * HS : place + (pair + 1) * HS] = state
        bonus = r[:, at].astype(F32) * k[:, at].astype(F32) * bonuses[pair * TOK : (pair + 1) * TOK]
        through = jnp.exp2(-cum_out[TOK - 1 :, at]) * passes[:1]
        out[0, DECAY + pair : DECAY + pair + 1] = through
        out[0, BONUS + pair : BONUS + pair + 1] = jnp.sum(bonus, axis=0, keepdims=True)


def combine_kernel(got, out, done):
    done[...] = jnp.zeros(done.shape, F32)
    first, second = got.at[0], got.at[1]
    for pair in range(HALF):
        rows = slice(pair * HS, (pair + 1) * HS)
        below = slice(PULL + pair * HS, PULL + (pair + 1) * HS)
        near = first[DECAY + pair : DECAY + pair + 1]
        far = second[DECAY + pair : DECAY + pair + 1]
        ends = far * first[rows] + second[rows]
        pulls = first[below] + near * second[below]
        bonus = first[BONUS + pair : BONUS + pair + 1] + second[BONUS + pair : BONUS + pair + 1]
        rest = cat(near * far, bonus, axis=0)
        for peer in range(BLOCKS):
            at = (pair * BLOCKS + peer) * ROWS_OUT
            for place, state in enumerate((ends, pulls)):
                row = at + place * STATE_ROWS
                out[row : row + STATE_ROWS] = state[peer * STATE_ROWS : (peer + 1) * STATE_ROWS]
            out[at + 2 * STATE_ROWS : at + ROWS_OUT] = rest


def expand_kernel(got, sums, before, out):
    del before
    first, second = sums.at[0], sums.at[1]
    for pair in range(HALF):
        rows = slice(pair * HS, (pair + 1) * HS)
        below = slice(PULL + pair * HS, PULL + (pair + 1) * HS)
        starts = [(pair * BLOCKS + peer) * ROWS_BACK for peer in range(BLOCKS)]
        state = cat(*(got[row : row + STATE_ROWS] for row in starts), axis=0)
        dstate = cat(*(got[row + STATE_ROWS : row + 2 * STATE_ROWS] for row in starts), axis=0)
        bonus = got[starts[0] + 2 * STATE_ROWS : starts[0] + ROWS_BACK]
        near = first[DECAY + pair : DECAY + pair + 1]
        far = second[DECAY + pair : DECAY + pair + 1]
        out[0, rows] = state
        out[0, below] = far * dstate + second[below]
        out[1, rows] = near * state + first[rows]
        out[1, below] = dstate
        for core in range(CORES):
            out[core, DECAY + pair : DECAY + pair + 1] = bonus


def scan_kernel(got, before, out, done):
    del before
    done[...] = jnp.zeros(done.shape, F32)
    shards = got.shape[0] // ROWS_OUT
    state = jnp.zeros((STATE_ROWS, LANES), F32)
    bonus = jnp.zeros((1, LANES), F32)
    for shard in range(shards):
        at, to = shard * ROWS_OUT, shard * ROWS_BACK
        out[to : to + STATE_ROWS] = state
        through = got[at + 2 * STATE_ROWS : at + 2 * STATE_ROWS + 1]
        state = through * state + got[at : at + STATE_ROWS]
        bonus = bonus + got[at + 2 * STATE_ROWS + 1 : at + ROWS_OUT]
    state = jnp.zeros((STATE_ROWS, LANES), F32)
    for shard in reversed(range(shards)):
        at, to = shard * ROWS_OUT, shard * ROWS_BACK
        out[to + STATE_ROWS : to + 2 * STATE_ROWS] = state
        out[to + 2 * STATE_ROWS : to + ROWS_BACK] = bonus
        through = got[at + 2 * STATE_ROWS : at + 2 * STATE_ROWS + 1]
        state = through * state + got[at + STATE_ROWS : at + 2 * STATE_ROWS]


def inside_kernel(r, k, v, g, x, cum_in, u, masks, combined, full_out, half_out, done):
    del combined
    done[...] = jnp.zeros(done.shape, F32)
    dr, dk, dv, dl, rd, kd, pr, pk, rate = (full_out.at[rows] for rows in FULL_ROWS)
    el, gc, vc = (half_out.at[rows] for rows in HALF_ROWS)
    through = full_out.at[FULL_TOK:]
    heads = head_masks()
    ones = ones_by_head()
    row, col = square()
    after = (row < col).astype(F32).astype(BF16)
    onward = -((row <= col).astype(F32).astype(BF16))
    sums = cat(after, onward, axis=1)
    allowed = cat(masks[0], masks[0], axis=1)
    later = cat(masks[1], masks[1], axis=1) > 0.0
    both = masks[2][TOK - 1 :] * masks[3][TOK - 1 :]
    spots = [slice(pair * LANES, (pair + 1) * LANES) for pair in range(r.shape[1] // LANES)]
    scaled, products = [], []
    for at in spots:
        rp, kp, vp, gp = (part[:, at].astype(F32) for part in (r, k, v, g))
        cum = cum_in[:, at]
        last = cum[TOK - 1 :]
        middle = 0.5 * last
        speed = decay_rate(x[:, at])
        scale_r = jnp.exp2(middle + (speed - cum))
        scale_k = jnp.exp2(cum - middle)
        scaled.append((scale_r, scale_k, halves(rp * scale_r), halves(kp * scale_k)))
        products += [cat(*halves(rp * u[:, at] * kp), axis=1), cat(*halves(gp * vp), axis=1)]
        reached = jnp.exp2(speed - cum) * masks[3]
        kept = jnp.exp2(cum - last) * masks[2]
        rd[:, at] = reached
        kd[:, at] = kept
        pr[:, at] = rp * reached
        ending = kp * kept
        pk[:, at] = ending
        el[:, at] = halves(ending)[1]
        rate[:, at] = -LN_2 * speed
        through[:, at] = jnp.broadcast_to(jnp.exp2(-last) * both, (8, LANES))
        gc[:, at] = g[:, at]
        vc[:, at] = v[:, at]
    own = dot(cat(*products, axis=0), ones, NN)
    pulls, scores = [], []
    for at, (_, _, (rh, rl), (kh, kl)) in zip(spots, scaled):
        g2 = by_head(g[:, at], heads)
        pulls.append(halves(side_by_side(dot(g2, v[:, at], NT)) * allowed))
        score = dot(cat(by_head(kh, heads), by_head(kl, heads), axis=1), cat(rh, rh, axis=1), NT)
        score = score + dot(by_head(kh, heads), rl, NT)
        scores.append(halves(jnp.where(later, side_by_side(score), 0.0)))
    flipped = [[cat(part[:, :TOK].T, part[:, TOK:].T, axis=1) for part in pull] for pull in pulls]
    paired = []
    for pair, at in enumerate(spots):
        scale_r, scale_k, (rh, rl), (kh, kl) = scaled[pair]
        rh2, rl2, kh2, kl2 = (by_head(part, heads) for part in (rh, rl, kh, kl))
        (ph, plow), (th, tl), (sh, sl) = pulls[pair], flipped[pair], scores[pair]
        g2 = by_head(g[:, at], heads)
        rp, kp, gp = (part[:, at].astype(F32) for part in (r, k, g))
        mine = own[2 * pair * TOK : (2 * pair + 1) * TOK]
        dot_gv = u[:, at] * own[(2 * pair + 1) * TOK : (2 * pair + 2) * TOK]
        dv[:, at] = dot(sh, g2, NN) + dot(sl, g2, NN) + mine * gp
        dri = scale_r * (dot(ph, kh2, NN) + dot(ph, kl2, NN) + dot(plow, kh2, NN))
        dki = scale_k * (dot(th, rh2, NN) + dot(th, rl2, NN) + dot(tl, rh2, NN))
        dr[:, at] = dri + dot_gv * kp
        dk[:, at] = dki + dot_gv * rp
        paired.append(cat(*halves(cat(rp * dri, kp * dki, axis=0)), axis=1))
    moved = [dot(sums, part, NN) for part in paired]
    for at, part in zip(spots, moved):
        dl[:, at] = part[:, :LANES] + part[:, LANES:]


def final_kernel(full_a, narrow_a, full_b, narrow_b, got, dr, dk, dv, dx, du, rounded, sems):
    heads = head_masks()
    row, col = square()
    after = (row < col).astype(F32).astype(BF16)
    earlier = (row > col).astype(F32).astype(BF16)
    sums = cat(after, earlier, axis=1)
    copies = []
    for base in range(0, du.shape[1] // LANES, WRITE):
        half = base // HALF
        full, narrow = ((full_a, narrow_a), (full_b, narrow_b))[half]
        dri, dki, dvi, dli, rd, kd, pr, pk, rate = (full.at[rows] for rows in FULL_ROWS)
        el_in, g, v = (narrow.at[rows] for rows in HALF_ROWS)
        places = range(base % HALF, base % HALF + WRITE)
        spots = [slice(place * LANES, (place + 1) * LANES) for place in places]
        targets = [slice(pair * LANES, (pair + 1) * LANES) for pair in range(base, base + WRITE)]
        loaded, across = [], []
        for place, at, to in zip(places, spots, targets):
            state = got[half, place * HS : (place + 1) * HS]
            dstate = got[half, PULL + place * HS : PULL + (place + 1) * HS]
            du[:, to] = got[half, DECAY + place : DECAY + place + 1]
            loaded.append([by_head(part, heads) for part in halves(state) + halves(dstate)])
            across.append(full[FULL_TOK : FULL_TOK + 1, at] * jnp.sum(state * dstate, axis=0, keepdims=True))
        reaches, pulls, values = [], [], []
        for at, (sh, sl, dh, dlow) in zip(spots, loaded):
            gb, vb = g[:, at], v[:, at]
            reaches.append(dot(cat(gb, gb, axis=1), cat(sh, sl, axis=0), NN))
            pulls.append(dot(cat(vb, vb, axis=1), cat(dh, dlow, axis=0), NN))
            eh, el = pk[:, at].astype(BF16), el_in[:, at]
            values.append(dot(cat(eh, el, axis=1), cat(dh, dh, axis=1), NT) + dot(eh, dlow, NT))
        paired = []
        for at, reach, pull in zip(spots, reaches, pulls):
            paired.append(cat(*halves(cat(pr[:, at] * reach, pk[:, at] * pull, axis=0)), axis=1))
        moved = [dot(sums, part, NN) for part in paired]
        for n, (at, to) in enumerate(zip(spots, targets)):
            rounded[0, :, to] = (dri[:, at] + rd[:, at] * reaches[n]).astype(BF16)
            rounded[1, :, to] = (dki[:, at] + kd[:, at] * pulls[n]).astype(BF16)
            rounded[2, :, to] = (dvi[:, at] + values[n]).astype(BF16)
            grad = dli[:, at] + moved[n][:, :LANES] + moved[n][:, LANES:] + across[n]
            rounded[3, :, to] = (rate[:, at] * grad).astype(BF16)
        ready = slice(base * LANES, (base + WRITE) * LANES)
        for n, out in enumerate((dr, dk, dv, dx)):
            copies.append(pltpu.make_async_copy(rounded.at[n, :, ready], out.at[:, ready], sems.at[base // WRITE, n]))
            copies[-1].start()
    for copy in copies:
        copy.wait()


def hbm(x):
    return pltpu.with_memory_space_constraint(x, pltpu.HBM)


def vm(x):
    return pltpu.with_memory_space_constraint(x, pltpu.VMEM)


def exchange(rows, peers, axis):
    packets = rows.reshape(peers, -1, 1, LANES)
    return lax.all_to_all(packets, axis, 0, 0, tiled=True).reshape(rows.shape)


def body(r, k, v, x, u, g, spans):
    tokens, width = r.shape
    npairs = width // LANES
    chips = lax.axis_size("chip")
    steps = npairs // PAIRS
    part = PAIRS * LANES
    r, k, v, x, g, u = (hbm(part) for part in (r, k, v, x, g, u.reshape(1, -1)))
    wide = pl.BlockSpec((TOK, part), lambda i: (0, i))
    thin = pl.BlockSpec((1, part), lambda i: (0, i))
    fixed = pl.BlockSpec((4, TOK, LANES), lambda i: (0, 0, 0))
    whole = pl.BlockSpec(memory_space=pltpu.VMEM)
    token = pl.BlockSpec(memory_space=pl.ANY)
    params = pltpu.CompilerParams(vmem_limit_bytes=VMEM)
    assert PAIRS == HALF

    def cost(flops, moved):
        return pl.CostEstimate(flops=flops, bytes_accessed=moved, transcendentals=0)

    def inside(half, after):
        part = INSIDE * LANES
        here = half * HALF // INSIDE
        wide = pl.BlockSpec((TOK, part), lambda i: (0, i + here))
        return pl.pallas_call(
            inside_kernel,
            grid=(HALF // INSIDE,),
            in_specs=[wide] * 6 + [pl.BlockSpec((1, part), lambda i: (0, i + here)), fixed, token],
            out_specs=[
                pl.BlockSpec((FULL_TOK + 8, part), lambda i: (0, i)),
                pl.BlockSpec((3 * TOK, part), lambda i: (0, i)),
                pl.BlockSpec((8, LANES), lambda i: (0, 0)),
            ],
            out_shape=[
                pltpu.HBM((FULL_TOK + 8, HALF * LANES), F32),
                pltpu.HBM((3 * TOK, HALF * LANES), BF16),
                pltpu.HBM((8, LANES), F32),
            ],
            name="inside",
            compiler_params=params,
            cost_estimate=cost(10**10, 10**7),
        )(r, k, v, g, x, hbm(cum), u, hbm(masks), hbm(after))

    summaries, cum, masks = pl.pallas_call(
        summary_kernel,
        grid=(steps,),
        in_specs=[pl.BlockSpec((1, spans.shape[0]), lambda i: (0, 0))] + [wide] * 5,
        out_specs=[pl.BlockSpec((1, BONUS + HALF, LANES), lambda i: (i, 0, 0)), wide, fixed],
        scratch_shapes=[
            pltpu.VMEM((TOK, LANES), F32),
            pltpu.VMEM((TOK, LANES), F32),
            pltpu.VMEM((8, LANES), F32),
        ],
        out_shape=[
            jax.ShapeDtypeStruct((CORES, BONUS + HALF, LANES), F32),
            pltpu.HBM((tokens, width), F32),
            pltpu.HBM((4, TOK, LANES), F32),
        ],
        name="summary",
        compiler_params=params,
        cost_estimate=cost(10**9, 6 * 10**6),
    )(hbm(spans.reshape(1, -1)), r, k, v, g, x)
    both = lax.all_to_all(summaries, "core", 0, 0, tiled=True)
    packets, combined = pl.pallas_call(
        combine_kernel,
        in_specs=[whole],
        out_specs=[whole, whole],
        out_shape=[jax.ShapeDtypeStruct((chips * ROWS_OUT, LANES), F32), pltpu.HBM((8, LANES), F32)],
        name="combine",
        compiler_params=params,
        cost_estimate=cost(10**6, 2 * 10**6),
    )(both)
    got = exchange(packets, chips, "chip")
    first, narrow_first, done = inside(0, combined)
    states, scanned = pl.pallas_call(
        scan_kernel,
        in_specs=[whole, token],
        out_specs=[whole, whole],
        out_shape=[jax.ShapeDtypeStruct((chips * ROWS_BACK, LANES), F32), pltpu.HBM((8, LANES), F32)],
        name="scan",
        compiler_params=params,
        cost_estimate=cost(10**10, 3 * 10**7),
    )(vm(got), hbm(done))
    returned = exchange(states, chips, "chip")
    second, narrow_second, done = inside(1, scanned)
    starts = pl.pallas_call(
        expand_kernel,
        in_specs=[whole, whole, token],
        out_specs=whole,
        out_shape=jax.ShapeDtypeStruct((CORES, BONUS, LANES), F32),
        name="expand",
        compiler_params=params,
        cost_estimate=cost(10**10, 3 * 10**7),
    )(returned, both, hbm(done))
    starts = lax.all_to_all(starts, "core", 0, 0, tiled=True)
    dr, dk, dv, dx, du = pl.pallas_call(
        final_kernel,
        in_specs=[whole] * 5,
        out_specs=[pl.BlockSpec(memory_space=pl.ANY)] * 4 + [whole],
        out_shape=[pltpu.HBM((tokens, width), BF16)] * 4 + [jax.ShapeDtypeStruct((1, width), F32)],
        scratch_shapes=[
            pltpu.VMEM((4, tokens, width), BF16),
            pltpu.SemaphoreType.DMA((npairs // WRITE, 4)),
        ],
        name="final",
        compiler_params=params,
        cost_estimate=cost(10**9, 10**7),
    )(vm(first), vm(narrow_first), vm(second), vm(narrow_second), vm(starts))
    return dr, dk, dv, dx, du.reshape(width)


def solution(mesh):
    chips = Mesh(mesh.devices.reshape(-1, CORES), ("chip", "core"))
    split, whole = P(("chip", "core"), None), P()
    return jax.shard_map(
        body,
        mesh=chips,
        in_specs=(split, split, split, split, whole, split, whole),
        out_specs=(split, split, split, split, whole),
        check_vma=False,
    )
```

```python
import jax
import jax.numpy as jnp
from jax import lax
from jax.experimental import pallas as pl
from jax.experimental.pallas import tpu as pltpu
from jax.sharding import Mesh
from jax.sharding import PartitionSpec as P

HS = 64
LANES = 128
TOK = 128
CORES = 2
HALF = 8
BLOCKS = 8
STATE_ROWS = HS // BLOCKS
ROWS_OUT = 18
ROWS_BACK = 17
PULL = HALF * HS
DECAY = 2 * PULL
BONUS = DECAY + HALF
GROUP = 4
INSIDE = 4
PAIRS = 8
VMEM = 24 * 2**20
WRITE = 4
LOG2_E = 1.4426950408889634
LOG2_LOG2_E = 0.5287663729448977
LN_2 = 0.6931471805599453
F32 = jnp.float32
BF16 = jnp.bfloat16

FULL_ROWS = [slice(n * TOK, (n + 1) * TOK) for n in range(9)]
FULL_TOK = 9 * TOK
HALF_ROWS = [slice(n * TOK, (n + 1) * TOK) for n in range(3)]

NN = (((1,), (0,)), ((), ()))
NT = (((1,), (1,)), ((), ()))
TN = (((0,), (0,)), ((), ()))


def dot(a, b, dims):
    return lax.dot_general(a, b, dims, preferred_element_type=F32)


def halves(x):
    high = x.astype(BF16)
    return high, (x - high.astype(F32)).astype(BF16)


def head_masks():
    lane = lax.broadcasted_iota(jnp.int32, (1, LANES), 1)
    return (lane < HS).astype(F32).astype(BF16), (lane >= HS).astype(F32).astype(BF16)


def by_head(x, masks):
    return jnp.concatenate([x * masks[0], x * masks[1]], axis=0)


def side_by_side(x):
    return jnp.concatenate([x[:TOK], x[TOK:]], axis=1)


def cat(*parts, axis):
    return jnp.concatenate(parts, axis=axis)


def square(n=TOK):
    row = lax.broadcasted_iota(jnp.int32, (n, n), 0)
    return row, lax.broadcasted_iota(jnp.int32, (n, n), 1)


def ones_by_head():
    row, col = square()
    same = ((row < HS) == (col < HS)).astype(F32).astype(BF16)
    return cat(same, same, axis=0)


def head_sums(x, ones):
    high, low = halves(x)
    return dot(cat(high, low, axis=1), ones, NN)


def segments(spans, base):
    ndocs = spans.shape[1]
    row, col = square(ndocs)
    upper = (row <= col).astype(F32).astype(BF16)
    spans = jnp.broadcast_to(spans, (8, ndocs))
    coarse, fine = ((part.astype(F32)).astype(BF16) for part in (spans >> 6, spans & 63))
    ends = (64.0 * dot(coarse, upper, NN) + dot(fine, upper, NN))[:1]
    down = (base + lax.broadcasted_iota(jnp.int32, (TOK, 1), 0)).astype(F32)
    seg_down = jnp.sum(jnp.where(ends <= down, 1.0, 0.0), axis=1, keepdims=True)
    row, col = square()
    seg_across = jnp.sum(jnp.where(row == col, seg_down, 0.0), axis=0, keepdims=True)
    prev = jnp.sum(jnp.where(ends <= down[:1] - 1.0, 1.0, 0.0), axis=1, keepdims=True)
    return seg_across, seg_down, jnp.where(down[:1] > 0.0, prev, -1.0)


def decay_rate(x):
    return jnp.exp2(x * LOG2_E + LOG2_LOG2_E)


def mark_segments(spans, marks):
    rank = lax.axis_index("chip") * CORES + lax.axis_index("core")
    seg_across, seg_down, prev = segments(spans[...], rank * TOK)
    row, col = square()
    same = seg_down == seg_across
    last = seg_down[TOK - 1 :]
    marks[0] = (same & (row > col)).astype(F32)
    marks[1] = (same & (row < col)).astype(F32)
    marks[2] = jnp.broadcast_to((seg_down == last).astype(F32), (TOK, LANES))
    marks[3] = jnp.broadcast_to((seg_down == prev).astype(F32), (TOK, LANES))


def running_sum(speeds):
    row, col = square()
    lower = (row >= col).astype(F32).astype(BF16)
    return dot(cat(lower, lower, axis=1), cat(*halves(speeds), axis=0), NN)


def summary_kernel(spans, r, k, v, g, x, mine, theirs, cums, marks, out):
    @pl.when(pl.program_id(0) == 0)
    def _():
        mark_segments(spans, marks)

    keep, carried = marks.at[2], marks.at[3]
    passes = marks[2, TOK - 1 :] * marks[3, TOK - 1 :]
    ones = ones_by_head()
    lane = lax.broadcasted_iota(jnp.int32, (HS, LANES), 1)
    spots = [slice(pair * LANES, (pair + 1) * LANES) for pair in range(PAIRS)]
    for group in range(0, PAIRS, GROUP):
        wide = slice(group * LANES, (group + GROUP) * LANES)
        cums[:, wide] = running_sum(decay_rate(x[:, wide]))
    products = [cat(*halves(g[:, at].astype(F32) * v[:, at].astype(F32)), axis=1) for at in spots]
    bonuses = dot(cat(*products, axis=0), ones, NN)
    endings, reaches = [], []
    for at in spots:
        cum = cums[:, at]
        rp, kp = r[:, at].astype(F32), k[:, at].astype(F32)
        ending = kp * jnp.exp2(cum - cum[TOK - 1 :]) * keep[...]
        reached = rp * jnp.exp2(decay_rate(x[:, at]) - cum) * carried[...]
        endings.append(cat(*halves(ending), axis=1))
        reaches.append(cat(*halves(reached), axis=1))
    ends = [dot(v[:, at], ending, TN) for at, ending in zip(spots, endings)]
    pulls = [dot(g[:, at], reached, TN) for at, reached in zip(spots, reaches)]
    for pair, at in enumerate(spots):
        for place, both in ((0, ends[pair]), (PULL, pulls[pair])):
            both = both[:, :LANES] + both[:, LANES:]
            state = jnp.where(lane < HS, both[:HS], both[HS:])
            out[place + pair * HS : place + (pair + 1) * HS] = state
        bonus = r[:, at].astype(F32) * k[:, at].astype(F32) * bonuses[pair * TOK : (pair + 1) * TOK]
        through = jnp.exp2(-cums[TOK - 1 :, at]) * passes
        out[DECAY + pair : DECAY + pair + 1] = through
        out[BONUS + pair : BONUS + pair + 1] = jnp.sum(bonus, axis=0, keepdims=True)
    ours = pl.program_id(0) == lax.axis_index("core")
    for condition, target in ((ours, mine), (jnp.logical_not(ours), theirs)):

        @pl.when(condition)
        def _():
            target[...] = out[...]


def in_order(mine, theirs):
    first = lax.axis_index("core") == 0

    def load(rows):
        own, other = mine[rows], theirs[rows]
        return jnp.where(first, own, other), jnp.where(first, other, own)

    return load


def combine_kernel(mine, theirs, out, done):
    done[...] = jnp.zeros(done.shape, F32)
    load = in_order(mine, theirs)
    for pair in range(HALF):
        first_end, second_end = load(slice(pair * HS, (pair + 1) * HS))
        first_pull, second_pull = load(slice(PULL + pair * HS, PULL + (pair + 1) * HS))
        near, far = load(slice(DECAY + pair, DECAY + pair + 1))
        ends = far * first_end + second_end
        pulls = first_pull + near * second_pull
        bonus = sum(load(slice(BONUS + pair, BONUS + pair + 1)))
        rest = cat(near * far, bonus, axis=0)
        for peer in range(BLOCKS):
            at = (pair * BLOCKS + peer) * ROWS_OUT
            for place, state in enumerate((ends, pulls)):
                row = at + place * STATE_ROWS
                out[row : row + STATE_ROWS] = state[peer * STATE_ROWS : (peer + 1) * STATE_ROWS]
            out[at + 2 * STATE_ROWS : at + ROWS_OUT] = rest


def expand_kernel(got, mine, theirs, before, own, other):
    del before
    load = in_order(mine, theirs)
    first = lax.axis_index("core") == 0
    for pair in range(HALF):
        rows = slice(pair * HS, (pair + 1) * HS)
        below = slice(PULL + pair * HS, PULL + (pair + 1) * HS)
        starts = [(pair * BLOCKS + peer) * ROWS_BACK for peer in range(BLOCKS)]
        state = cat(*(got[row : row + STATE_ROWS] for row in starts), axis=0)
        dstate = cat(*(got[row + STATE_ROWS : row + 2 * STATE_ROWS] for row in starts), axis=0)
        bonus = got[starts[0] + 2 * STATE_ROWS : starts[0] + ROWS_BACK]
        near, far = load(slice(DECAY + pair, DECAY + pair + 1))
        second_state = near * state + load(rows)[0]
        first_dstate = far * dstate + load(below)[1]
        own[rows] = jnp.where(first, state, second_state)
        other[rows] = jnp.where(first, second_state, state)
        own[below] = jnp.where(first, first_dstate, dstate)
        other[below] = jnp.where(first, dstate, first_dstate)
        for out in (own, other):
            out[DECAY + pair : DECAY + pair + 1] = bonus


def scan_kernel(got, before, out, done):
    del before
    done[...] = jnp.zeros(done.shape, F32)
    shards = got.shape[0] // ROWS_OUT
    state = jnp.zeros((STATE_ROWS, LANES), F32)
    bonus = jnp.zeros((1, LANES), F32)
    for shard in range(shards):
        at, to = shard * ROWS_OUT, shard * ROWS_BACK
        out[to : to + STATE_ROWS] = state
        through = got[at + 2 * STATE_ROWS : at + 2 * STATE_ROWS + 1]
        state = through * state + got[at : at + STATE_ROWS]
        bonus = bonus + got[at + 2 * STATE_ROWS + 1 : at + ROWS_OUT]
    state = jnp.zeros((STATE_ROWS, LANES), F32)
    for shard in reversed(range(shards)):
        at, to = shard * ROWS_OUT, shard * ROWS_BACK
        out[to + STATE_ROWS : to + 2 * STATE_ROWS] = state
        out[to + 2 * STATE_ROWS : to + ROWS_BACK] = bonus
        through = got[at + 2 * STATE_ROWS : at + 2 * STATE_ROWS + 1]
        state = through * state + got[at + STATE_ROWS : at + 2 * STATE_ROWS]


def inside_kernel(spans, r, k, v, g, x, u, before, full_out, half_out, done, cums, masks):
    del before

    @pl.when(pl.program_id(0) == 0)
    def _():
        mark_segments(spans, masks)

    done[...] = jnp.zeros(done.shape, F32)
    dr, dk, dv, dl, rd, kd, pr, pk, rate = (full_out.at[rows] for rows in FULL_ROWS)
    el, gc, vc = (half_out.at[rows] for rows in HALF_ROWS)
    through = full_out.at[FULL_TOK:]
    heads = head_masks()
    ones = ones_by_head()
    row, col = square()
    after = (row < col).astype(F32).astype(BF16)
    onward = -((row <= col).astype(F32).astype(BF16))
    sums = cat(after, onward, axis=1)
    allowed = cat(masks[0], masks[0], axis=1)
    later = cat(masks[1], masks[1], axis=1) > 0.0
    both = masks[2][TOK - 1 :] * masks[3][TOK - 1 :]
    spots = [slice(pair * LANES, (pair + 1) * LANES) for pair in range(r.shape[1] // LANES)]
    cums[...] = running_sum(decay_rate(x[...]))
    scaled, products = [], []
    for at in spots:
        rp, kp, vp, gp = (part[:, at].astype(F32) for part in (r, k, v, g))
        cum = cums[:, at]
        last = cum[TOK - 1 :]
        middle = 0.5 * last
        speed = decay_rate(x[:, at])
        scale_r = jnp.exp2(middle + (speed - cum))
        scale_k = jnp.exp2(cum - middle)
        scaled.append((scale_r, scale_k, halves(rp * scale_r), halves(kp * scale_k)))
        products += [cat(*halves(rp * u[:, at] * kp), axis=1), cat(*halves(gp * vp), axis=1)]
        reached = jnp.exp2(speed - cum) * masks[3]
        kept = jnp.exp2(cum - last) * masks[2]
        rd[:, at] = reached
        kd[:, at] = kept
        pr[:, at] = rp * reached
        ending = kp * kept
        pk[:, at] = ending
        el[:, at] = halves(ending)[1]
        rate[:, at] = -LN_2 * speed
        through[:, at] = jnp.broadcast_to(jnp.exp2(-last) * both, (8, LANES))
        gc[:, at] = g[:, at]
        vc[:, at] = v[:, at]
    own = dot(cat(*products, axis=0), ones, NN)
    pulls, scores = [], []
    for at, (_, _, (rh, rl), (kh, kl)) in zip(spots, scaled):
        g2 = by_head(g[:, at], heads)
        pulls.append(halves(side_by_side(dot(g2, v[:, at], NT)) * allowed))
        score = dot(cat(by_head(kh, heads), by_head(kl, heads), axis=1), cat(rh, rh, axis=1), NT)
        score = score + dot(by_head(kh, heads), rl, NT)
        scores.append(halves(jnp.where(later, side_by_side(score), 0.0)))
    flipped = [[cat(part[:, :TOK].T, part[:, TOK:].T, axis=1) for part in pull] for pull in pulls]
    paired = []
    for pair, at in enumerate(spots):
        scale_r, scale_k, (rh, rl), (kh, kl) = scaled[pair]
        rh2, rl2, kh2, kl2 = (by_head(part, heads) for part in (rh, rl, kh, kl))
        (ph, plow), (th, tl), (sh, sl) = pulls[pair], flipped[pair], scores[pair]
        g2 = by_head(g[:, at], heads)
        rp, kp, gp = (part[:, at].astype(F32) for part in (r, k, g))
        mine = own[2 * pair * TOK : (2 * pair + 1) * TOK]
        dot_gv = u[:, at] * own[(2 * pair + 1) * TOK : (2 * pair + 2) * TOK]
        dv[:, at] = dot(sh, g2, NN) + dot(sl, g2, NN) + mine * gp
        dri = scale_r * (dot(ph, kh2, NN) + dot(ph, kl2, NN) + dot(plow, kh2, NN))
        dki = scale_k * (dot(th, rh2, NN) + dot(th, rl2, NN) + dot(tl, rh2, NN))
        dr[:, at] = dri + dot_gv * kp
        dk[:, at] = dki + dot_gv * rp
        paired.append(cat(*halves(cat(rp * dri, kp * dki, axis=0)), axis=1))
    moved = [dot(sums, part, NN) for part in paired]
    for at, part in zip(spots, moved):
        dl[:, at] = part[:, :LANES] + part[:, LANES:]


def final_kernel(full_a, narrow_a, full_b, narrow_b, mine, theirs, dr, dk, dv, dx, du, rounded, sems):
    heads = head_masks()
    row, col = square()
    after = (row < col).astype(F32).astype(BF16)
    earlier = (row > col).astype(F32).astype(BF16)
    sums = cat(after, earlier, axis=1)
    load = in_order(mine, theirs)
    got = (lambda rows: load(rows)[0], lambda rows: load(rows)[1])
    copies = []
    for base in range(0, du.shape[1] // LANES, WRITE):
        half = base // HALF
        full, narrow = ((full_a, narrow_a), (full_b, narrow_b))[half]
        dri, dki, dvi, dli, rd, kd, pr, pk, rate = (full.at[rows] for rows in FULL_ROWS)
        el_in, g, v = (narrow.at[rows] for rows in HALF_ROWS)
        places = range(base % HALF, base % HALF + WRITE)
        spots = [slice(place * LANES, (place + 1) * LANES) for place in places]
        targets = [slice(pair * LANES, (pair + 1) * LANES) for pair in range(base, base + WRITE)]
        loaded, across = [], []
        for place, at, to in zip(places, spots, targets):
            state = got[half](slice(place * HS, (place + 1) * HS))
            dstate = got[half](slice(PULL + place * HS, PULL + (place + 1) * HS))
            du[:, to] = got[half](slice(DECAY + place, DECAY + place + 1))
            loaded.append([by_head(part, heads) for part in halves(state) + halves(dstate)])
            across.append(full[FULL_TOK : FULL_TOK + 1, at] * jnp.sum(state * dstate, axis=0, keepdims=True))
        reaches, pulls, values = [], [], []
        for at, (sh, sl, dh, dlow) in zip(spots, loaded):
            gb, vb = g[:, at], v[:, at]
            reaches.append(dot(cat(gb, gb, axis=1), cat(sh, sl, axis=0), NN))
            pulls.append(dot(cat(vb, vb, axis=1), cat(dh, dlow, axis=0), NN))
            eh, el = pk[:, at].astype(BF16), el_in[:, at]
            values.append(dot(cat(eh, el, axis=1), cat(dh, dh, axis=1), NT) + dot(eh, dlow, NT))
        paired = []
        for at, reach, pull in zip(spots, reaches, pulls):
            paired.append(cat(*halves(cat(pr[:, at] * reach, pk[:, at] * pull, axis=0)), axis=1))
        moved = [dot(sums, part, NN) for part in paired]
        for n, (at, to) in enumerate(zip(spots, targets)):
            rounded[0, :, to] = (dri[:, at] + rd[:, at] * reaches[n]).astype(BF16)
            rounded[1, :, to] = (dki[:, at] + kd[:, at] * pulls[n]).astype(BF16)
            rounded[2, :, to] = (dvi[:, at] + values[n]).astype(BF16)
            grad = dli[:, at] + moved[n][:, :LANES] + moved[n][:, LANES:] + across[n]
            rounded[3, :, to] = (rate[:, at] * grad).astype(BF16)
        ready = slice(base * LANES, (base + WRITE) * LANES)
        for n, out in enumerate((dr, dk, dv, dx)):
            copies.append(pltpu.make_async_copy(rounded.at[n, :, ready], out.at[:, ready], sems.at[base // WRITE, n]))
            copies[-1].start()
    for copy in copies:
        copy.wait()


def hbm(x):
    return pltpu.with_memory_space_constraint(x, pltpu.HBM)


def vm(x):
    return pltpu.with_memory_space_constraint(x, pltpu.VMEM)


def swap(rows):
    return lax.ppermute(rows, "core", [(0, 1), (1, 0)])


def exchange(rows, peers, axis):
    packets = rows.reshape(peers, -1, 1, LANES)
    return lax.all_to_all(packets, axis, 0, 0, tiled=True).reshape(rows.shape)


def body(r, k, v, x, u, g, spans):
    tokens, width = r.shape
    npairs = width // LANES
    chips = lax.axis_size("chip")
    r, k, v, x, g, u = (hbm(part) for part in (r, k, v, x, g, u.reshape(1, -1)))
    spans = hbm(spans.reshape(1, -1))
    whole = pl.BlockSpec(memory_space=pltpu.VMEM)
    token = pl.BlockSpec(memory_space=pl.ANY)
    params = pltpu.CompilerParams(vmem_limit_bytes=VMEM)
    assert PAIRS == HALF

    def cost(flops, moved):
        return pl.CostEstimate(flops=flops, bytes_accessed=moved, transcendentals=0)

    def inside(half, after):
        part = INSIDE * LANES
        here = half * HALF // INSIDE
        wide = pl.BlockSpec((TOK, part), lambda i: (0, i + here))
        return pl.pallas_call(
            inside_kernel,
            grid=(HALF // INSIDE,),
            in_specs=[whole] + [wide] * 5 + [pl.BlockSpec((1, part), lambda i: (0, i + here)), token],
            out_specs=[
                pl.BlockSpec((FULL_TOK + 8, part), lambda i: (0, i)),
                pl.BlockSpec((3 * TOK, part), lambda i: (0, i)),
                pl.BlockSpec((8, LANES), lambda i: (0, 0)),
            ],
            out_shape=[
                pltpu.HBM((FULL_TOK + 8, HALF * LANES), F32),
                pltpu.HBM((3 * TOK, HALF * LANES), BF16),
                pltpu.HBM((8, LANES), F32),
            ],
            scratch_shapes=[pltpu.VMEM((TOK, part), F32), pltpu.VMEM((4, TOK, LANES), F32)],
            name="inside",
            compiler_params=params,
            cost_estimate=cost(10**10, 10**7),
        )(spans, r, k, v, g, x, u, hbm(after))

    part = PAIRS * LANES
    block = (BONUS + HALF, LANES)
    mine, theirs = pl.pallas_call(
        summary_kernel,
        grid=(width // part,),
        in_specs=[whole] + [pl.BlockSpec((TOK, part), lambda i: (0, i))] * 5,
        out_specs=[whole] * 2,
        out_shape=[jax.ShapeDtypeStruct(block, F32)] * 2,
        scratch_shapes=[
            pltpu.VMEM((TOK, part), F32),
            pltpu.VMEM((4, TOK, LANES), F32),
            pltpu.VMEM(block, F32),
        ],
        name="summary",
        compiler_params=params,
        cost_estimate=cost(10**9, 6 * 10**6),
    )(spans, r, k, v, g, x)
    theirs = swap(theirs)
    packets, combined = pl.pallas_call(
        combine_kernel,
        in_specs=[whole] * 2,
        out_specs=[whole, whole],
        out_shape=[jax.ShapeDtypeStruct((chips * ROWS_OUT, LANES), F32), pltpu.HBM((8, LANES), F32)],
        name="combine",
        compiler_params=params,
        cost_estimate=cost(10**6, 2 * 10**6),
    )(mine, theirs)
    got = exchange(packets, chips, "chip")
    first, narrow_first, done = inside(0, combined)
    states, scanned = pl.pallas_call(
        scan_kernel,
        in_specs=[whole, token],
        out_specs=[whole, whole],
        out_shape=[jax.ShapeDtypeStruct((chips * ROWS_BACK, LANES), F32), pltpu.HBM((8, LANES), F32)],
        name="scan",
        compiler_params=params,
        cost_estimate=cost(10**10, 3 * 10**7),
    )(vm(got), hbm(done))
    returned = exchange(states, chips, "chip")
    second, narrow_second, done = inside(1, scanned)
    own, other = pl.pallas_call(
        expand_kernel,
        in_specs=[whole, whole, whole, token],
        out_specs=[whole] * 2,
        out_shape=[jax.ShapeDtypeStruct((BONUS, LANES), F32)] * 2,
        name="expand",
        compiler_params=params,
        cost_estimate=cost(10**10, 3 * 10**7),
    )(returned, mine, theirs, hbm(done))
    other = swap(other)
    dr, dk, dv, dx, du = pl.pallas_call(
        final_kernel,
        in_specs=[whole] * 6,
        out_specs=[pl.BlockSpec(memory_space=pl.ANY)] * 4 + [whole],
        out_shape=[pltpu.HBM((tokens, width), BF16)] * 4 + [jax.ShapeDtypeStruct((1, width), F32)],
        scratch_shapes=[
            pltpu.VMEM((4, tokens, width), BF16),
            pltpu.SemaphoreType.DMA((npairs // WRITE, 4)),
        ],
        name="final",
        compiler_params=params,
        cost_estimate=cost(10**9, 10**7),
    )(vm(first), vm(narrow_first), vm(second), vm(narrow_second), vm(own), vm(other))
    return dr, dk, dv, dx, du.reshape(width)


def solution(mesh):
    chips = Mesh(mesh.devices.reshape(-1, CORES), ("chip", "core"))
    split, whole = P(("chip", "core"), None), P()
    return jax.shard_map(
        body,
        mesh=chips,
        in_specs=(split, split, split, split, whole, split, whole),
        out_specs=(split, split, split, split, whole),
        check_vma=False,
    )
```

```python
import jax
import jax.numpy as jnp
from jax import lax
from jax.experimental import pallas as pl
from jax.experimental.pallas import tpu as pltpu
from jax.sharding import Mesh
from jax.sharding import PartitionSpec as P

HS = 64
LANES = 128
TOK = 128
CORES = 2
HALF = 8
BLOCKS = 8
STATE_ROWS = HS // BLOCKS
ROWS_OUT = 18
ROWS_BACK = 17
PULL = HALF * HS
DECAY = 2 * PULL
BONUS = DECAY + HALF
GROUP = 4
INSIDE = 4
PAIRS = 8
VMEM = 24 * 2**20
WRITE = 4
LOG2_E = 1.4426950408889634
LOG2_LOG2_E = 0.5287663729448977
LN_2 = 0.6931471805599453
F32 = jnp.float32
BF16 = jnp.bfloat16

FULL_ROWS = [slice(n * TOK, (n + 1) * TOK) for n in range(7)]
FULL_TOK = 7 * TOK

NN = (((1,), (0,)), ((), ()))
NT = (((1,), (1,)), ((), ()))
TN = (((0,), (0,)), ((), ()))


def dot(a, b, dims):
    return lax.dot_general(a, b, dims, preferred_element_type=F32)


def halves(x):
    high = x.astype(BF16)
    return high, (x - high.astype(F32)).astype(BF16)


def head_masks():
    lane = lax.broadcasted_iota(jnp.int32, (1, LANES), 1)
    return (lane < HS).astype(F32).astype(BF16), (lane >= HS).astype(F32).astype(BF16)


def by_head(x, masks):
    return jnp.concatenate([x * masks[0], x * masks[1]], axis=0)


def side_by_side(x):
    return jnp.concatenate([x[:TOK], x[TOK:]], axis=1)


def cat(*parts, axis):
    return jnp.concatenate(parts, axis=axis)


def square(n=TOK):
    row = lax.broadcasted_iota(jnp.int32, (n, n), 0)
    return row, lax.broadcasted_iota(jnp.int32, (n, n), 1)


def ones_by_head():
    row, col = square()
    same = ((row < HS) == (col < HS)).astype(F32).astype(BF16)
    return cat(same, same, axis=0)


def head_sums(x, ones):
    high, low = halves(x)
    return dot(cat(high, low, axis=1), ones, NN)


def segments(spans, base):
    ndocs = spans.shape[1]
    row, col = square(ndocs)
    upper = (row <= col).astype(F32).astype(BF16)
    spans = jnp.broadcast_to(spans, (8, ndocs))
    coarse, fine = ((part.astype(F32)).astype(BF16) for part in (spans >> 6, spans & 63))
    ends = (64.0 * dot(coarse, upper, NN) + dot(fine, upper, NN))[:1]
    down = (base + lax.broadcasted_iota(jnp.int32, (TOK, 1), 0)).astype(F32)
    seg_down = jnp.sum(jnp.where(ends <= down, 1.0, 0.0), axis=1, keepdims=True)
    row, col = square()
    seg_across = jnp.sum(jnp.where(row == col, seg_down, 0.0), axis=0, keepdims=True)
    prev = jnp.sum(jnp.where(ends <= down[:1] - 1.0, 1.0, 0.0), axis=1, keepdims=True)
    return seg_across, seg_down, jnp.where(down[:1] > 0.0, prev, -1.0)


def decay_rate(x):
    return jnp.exp2(x * LOG2_E + LOG2_LOG2_E)


def mark_segments(spans, marks):
    rank = lax.axis_index("chip") * CORES + lax.axis_index("core")
    seg_across, seg_down, prev = segments(spans[...], rank * TOK)
    row, col = square()
    same = seg_down == seg_across
    last = seg_down[TOK - 1 :]
    marks[0] = (same & (row > col)).astype(F32)
    marks[1] = (same & (row < col)).astype(F32)
    marks[2] = jnp.broadcast_to((seg_down == last).astype(F32), (TOK, LANES))
    marks[3] = jnp.broadcast_to((seg_down == prev).astype(F32), (TOK, LANES))


def running_sum(speeds):
    row, col = square()
    lower = (row >= col).astype(F32).astype(BF16)
    return dot(cat(lower, lower, axis=1), cat(*halves(speeds), axis=0), NN)


def summary_kernel(spans, r, k, v, g, x, mine, theirs, cums, marks, out):
    @pl.when(pl.program_id(0) == 0)
    def _():
        mark_segments(spans, marks)

    keep, carried = marks.at[2], marks.at[3]
    passes = marks[2, TOK - 1 :] * marks[3, TOK - 1 :]
    ones = ones_by_head()
    lane = lax.broadcasted_iota(jnp.int32, (HS, LANES), 1)
    spots = [slice(pair * LANES, (pair + 1) * LANES) for pair in range(PAIRS)]
    for group in range(0, PAIRS, GROUP):
        wide = slice(group * LANES, (group + GROUP) * LANES)
        cums[:, wide] = running_sum(decay_rate(x[:, wide]))
    products = [cat(*halves(g[:, at].astype(F32) * v[:, at].astype(F32)), axis=1) for at in spots]
    bonuses = dot(cat(*products, axis=0), ones, NN)
    endings, reaches = [], []
    for at in spots:
        cum = cums[:, at]
        rp, kp = r[:, at].astype(F32), k[:, at].astype(F32)
        ending = kp * jnp.exp2(cum - cum[TOK - 1 :]) * keep[...]
        reached = rp * jnp.exp2(decay_rate(x[:, at]) - cum) * carried[...]
        endings.append(cat(*halves(ending), axis=1))
        reaches.append(cat(*halves(reached), axis=1))
    ends = [dot(v[:, at], ending, TN) for at, ending in zip(spots, endings)]
    pulls = [dot(g[:, at], reached, TN) for at, reached in zip(spots, reaches)]
    for pair, at in enumerate(spots):
        for place, both in ((0, ends[pair]), (PULL, pulls[pair])):
            both = both[:, :LANES] + both[:, LANES:]
            state = jnp.where(lane < HS, both[:HS], both[HS:])
            out[place + pair * HS : place + (pair + 1) * HS] = state
        bonus = r[:, at].astype(F32) * k[:, at].astype(F32) * bonuses[pair * TOK : (pair + 1) * TOK]
        through = jnp.exp2(-cums[TOK - 1 :, at]) * passes
        out[DECAY + pair : DECAY + pair + 1] = through
        out[BONUS + pair : BONUS + pair + 1] = jnp.sum(bonus, axis=0, keepdims=True)
    ours = pl.program_id(0) == lax.axis_index("core")
    for condition, target in ((ours, mine), (jnp.logical_not(ours), theirs)):

        @pl.when(condition)
        def _():
            target[...] = out[...]


def in_order(mine, theirs):
    first = lax.axis_index("core") == 0

    def load(rows):
        own, other = mine[rows], theirs[rows]
        return jnp.where(first, own, other), jnp.where(first, other, own)

    return load


def combine_kernel(mine, theirs, out, done):
    done[...] = jnp.zeros(done.shape, F32)
    load = in_order(mine, theirs)
    for pair in range(HALF):
        first_end, second_end = load(slice(pair * HS, (pair + 1) * HS))
        first_pull, second_pull = load(slice(PULL + pair * HS, PULL + (pair + 1) * HS))
        near, far = load(slice(DECAY + pair, DECAY + pair + 1))
        ends = far * first_end + second_end
        pulls = first_pull + near * second_pull
        bonus = sum(load(slice(BONUS + pair, BONUS + pair + 1)))
        rest = cat(near * far, bonus, axis=0)
        for peer in range(BLOCKS):
            at = (pair * BLOCKS + peer) * ROWS_OUT
            for place, state in enumerate((ends, pulls)):
                row = at + place * STATE_ROWS
                out[row : row + STATE_ROWS] = state[peer * STATE_ROWS : (peer + 1) * STATE_ROWS]
            out[at + 2 * STATE_ROWS : at + ROWS_OUT] = rest


def expand_kernel(got, mine, theirs, before, own, other):
    del before
    load = in_order(mine, theirs)
    first = lax.axis_index("core") == 0
    for pair in range(HALF):
        rows = slice(pair * HS, (pair + 1) * HS)
        below = slice(PULL + pair * HS, PULL + (pair + 1) * HS)
        starts = [(pair * BLOCKS + peer) * ROWS_BACK for peer in range(BLOCKS)]
        state = cat(*(got[row : row + STATE_ROWS] for row in starts), axis=0)
        dstate = cat(*(got[row + STATE_ROWS : row + 2 * STATE_ROWS] for row in starts), axis=0)
        bonus = got[starts[0] + 2 * STATE_ROWS : starts[0] + ROWS_BACK]
        near, far = load(slice(DECAY + pair, DECAY + pair + 1))
        second_state = near * state + load(rows)[0]
        first_dstate = far * dstate + load(below)[1]
        own[rows] = jnp.where(first, state, second_state)
        other[rows] = jnp.where(first, second_state, state)
        own[below] = jnp.where(first, first_dstate, dstate)
        other[below] = jnp.where(first, dstate, first_dstate)
        for out in (own, other):
            out[DECAY + pair : DECAY + pair + 1] = bonus


def scan_kernel(got, before, out, done):
    del before
    done[...] = jnp.zeros(done.shape, F32)
    shards = got.shape[0] // ROWS_OUT
    state = jnp.zeros((STATE_ROWS, LANES), F32)
    bonus = jnp.zeros((1, LANES), F32)
    for shard in range(shards):
        at, to = shard * ROWS_OUT, shard * ROWS_BACK
        out[to : to + STATE_ROWS] = state
        through = got[at + 2 * STATE_ROWS : at + 2 * STATE_ROWS + 1]
        state = through * state + got[at : at + STATE_ROWS]
        bonus = bonus + got[at + 2 * STATE_ROWS + 1 : at + ROWS_OUT]
    state = jnp.zeros((STATE_ROWS, LANES), F32)
    for shard in reversed(range(shards)):
        at, to = shard * ROWS_OUT, shard * ROWS_BACK
        out[to + STATE_ROWS : to + 2 * STATE_ROWS] = state
        out[to + 2 * STATE_ROWS : to + ROWS_BACK] = bonus
        through = got[at + 2 * STATE_ROWS : at + 2 * STATE_ROWS + 1]
        state = through * state + got[at + STATE_ROWS : at + 2 * STATE_ROWS]


def inside_kernel(spans, r, k, v, g, x, u, before, full_out, kept, done, cums, masks):
    del before

    @pl.when(pl.program_id(0) == 0)
    def _():
        mark_segments(spans, masks)

    done[...] = jnp.zeros(done.shape, F32)
    dr, dk, dv, dl, rd, kd, rate = (full_out.at[rows] for rows in FULL_ROWS)
    through = full_out.at[FULL_TOK:]
    heads = head_masks()
    ones = ones_by_head()
    row, col = square()
    after = (row < col).astype(F32).astype(BF16)
    onward = -((row <= col).astype(F32).astype(BF16))
    sums = cat(after, onward, axis=1)
    allowed = cat(masks[0], masks[0], axis=1)
    later = cat(masks[1], masks[1], axis=1) > 0.0
    both = masks[2][TOK - 1 :] * masks[3][TOK - 1 :]
    spots = [slice(pair * LANES, (pair + 1) * LANES) for pair in range(r.shape[1] // LANES)]
    cums[...] = running_sum(decay_rate(x[...]))
    scaled, products = [], []
    for at in spots:
        rp, kp, vp, gp = (part[:, at].astype(F32) for part in (r, k, v, g))
        cum = cums[:, at]
        last = cum[TOK - 1 :]
        middle = 0.5 * last
        speed = decay_rate(x[:, at])
        scale_r = jnp.exp2(middle + (speed - cum))
        scale_k = jnp.exp2(cum - middle)
        scaled.append((scale_r, scale_k, halves(rp * scale_r), halves(kp * scale_k)))
        products += [cat(*halves(rp * u[:, at] * kp), axis=1), cat(*halves(gp * vp), axis=1)]
        rd[:, at] = jnp.exp2(speed - cum) * masks[3]
        kd[:, at] = jnp.exp2(cum - last) * masks[2]
        rate[:, at] = -LN_2 * speed
        through[:, at] = jnp.broadcast_to(jnp.exp2(-last) * both, (8, LANES))
        for n, stream in enumerate((r, k, v, g)):
            kept[n * TOK : (n + 1) * TOK, at] = stream[:, at]
    own = dot(cat(*products, axis=0), ones, NN)
    pulls, scores = [], []
    for at, (_, _, (rh, rl), (kh, kl)) in zip(spots, scaled):
        g2 = by_head(g[:, at], heads)
        pulls.append(halves(side_by_side(dot(g2, v[:, at], NT)) * allowed))
        score = dot(cat(by_head(kh, heads), by_head(kl, heads), axis=1), cat(rh, rh, axis=1), NT)
        score = score + dot(by_head(kh, heads), rl, NT)
        scores.append(halves(jnp.where(later, side_by_side(score), 0.0)))
    flipped = [[cat(part[:, :TOK].T, part[:, TOK:].T, axis=1) for part in pull] for pull in pulls]
    paired = []
    for pair, at in enumerate(spots):
        scale_r, scale_k, (rh, rl), (kh, kl) = scaled[pair]
        rh2, rl2, kh2, kl2 = (by_head(part, heads) for part in (rh, rl, kh, kl))
        (ph, plow), (th, tl), (sh, sl) = pulls[pair], flipped[pair], scores[pair]
        g2 = by_head(g[:, at], heads)
        rp, kp, gp = (part[:, at].astype(F32) for part in (r, k, g))
        mine = own[2 * pair * TOK : (2 * pair + 1) * TOK]
        dot_gv = u[:, at] * own[(2 * pair + 1) * TOK : (2 * pair + 2) * TOK]
        dv[:, at] = dot(sh, g2, NN) + dot(sl, g2, NN) + mine * gp
        dri = scale_r * (dot(ph, kh2, NN) + dot(ph, kl2, NN) + dot(plow, kh2, NN))
        dki = scale_k * (dot(th, rh2, NN) + dot(th, rl2, NN) + dot(tl, rh2, NN))
        dr[:, at] = dri + dot_gv * kp
        dk[:, at] = dki + dot_gv * rp
        paired.append(cat(*halves(cat(rp * dri, kp * dki, axis=0)), axis=1))
    moved = [dot(sums, part, NN) for part in paired]
    for at, part in zip(spots, moved):
        dl[:, at] = part[:, :LANES] + part[:, LANES:]


def final_kernel(full_a, kept_a, full_b, kept_b, mine, theirs, dr, dk, dv, dx, du, rounded, sems):
    heads = head_masks()
    row, col = square()
    after = (row < col).astype(F32).astype(BF16)
    earlier = (row > col).astype(F32).astype(BF16)
    sums = cat(after, earlier, axis=1)
    load = in_order(mine, theirs)
    got = (lambda rows: load(rows)[0], lambda rows: load(rows)[1])
    copies = []
    for base in range(0, du.shape[1] // LANES, WRITE):
        half = base // HALF
        full, kept = ((full_a, kept_a), (full_b, kept_b))[half]
        r, k, v, g = (kept.at[n * TOK : (n + 1) * TOK] for n in range(4))
        dri, dki, dvi, dli, rd, kd, rate = (full.at[rows] for rows in FULL_ROWS)
        places = range(base % HALF, base % HALF + WRITE)
        spots = [slice(place * LANES, (place + 1) * LANES) for place in places]
        targets = [slice(pair * LANES, (pair + 1) * LANES) for pair in range(base, base + WRITE)]
        loaded, across = [], []
        for place, at, to in zip(places, spots, targets):
            state = got[half](slice(place * HS, (place + 1) * HS))
            dstate = got[half](slice(PULL + place * HS, PULL + (place + 1) * HS))
            du[:, to] = got[half](slice(DECAY + place, DECAY + place + 1))
            loaded.append([by_head(part, heads) for part in halves(state) + halves(dstate)])
            across.append(full[FULL_TOK : FULL_TOK + 1, at] * jnp.sum(state * dstate, axis=0, keepdims=True))
        reaches, pulls, values, paired = [], [], [], []
        for at, (sh, sl, dh, dlow) in zip(spots, loaded):
            gb, vb = g[:, at], v[:, at]
            reaches.append(rd[:, at] * dot(cat(gb, gb, axis=1), cat(sh, sl, axis=0), NN))
            pulls.append(kd[:, at] * dot(cat(vb, vb, axis=1), cat(dh, dlow, axis=0), NN))
            eh, el = halves(k[:, at].astype(F32) * kd[:, at])
            values.append(dot(cat(eh, el, axis=1), cat(dh, dh, axis=1), NT) + dot(eh, dlow, NT))
        for at, reach, pull in zip(spots, reaches, pulls):
            rp, kp = r[:, at].astype(F32), k[:, at].astype(F32)
            paired.append(cat(*halves(cat(rp * reach, kp * pull, axis=0)), axis=1))
        moved = [dot(sums, part, NN) for part in paired]
        for n, (at, to) in enumerate(zip(spots, targets)):
            rounded[0, :, to] = (dri[:, at] + reaches[n]).astype(BF16)
            rounded[1, :, to] = (dki[:, at] + pulls[n]).astype(BF16)
            rounded[2, :, to] = (dvi[:, at] + values[n]).astype(BF16)
            grad = dli[:, at] + moved[n][:, :LANES] + moved[n][:, LANES:] + across[n]
            rounded[3, :, to] = (rate[:, at] * grad).astype(BF16)
        ready = slice(base * LANES, (base + WRITE) * LANES)
        for n, out in enumerate((dr, dk, dv, dx)):
            copies.append(pltpu.make_async_copy(rounded.at[n, :, ready], out.at[:, ready], sems.at[base // WRITE, n]))
            copies[-1].start()
    for copy in copies:
        copy.wait()


def hbm(x):
    return pltpu.with_memory_space_constraint(x, pltpu.HBM)


def vm(x):
    return pltpu.with_memory_space_constraint(x, pltpu.VMEM)


def swap(rows):
    return lax.ppermute(rows, "core", [(0, 1), (1, 0)])


def exchange(rows, peers, axis):
    packets = rows.reshape(peers, -1, 1, LANES)
    return lax.all_to_all(packets, axis, 0, 0, tiled=True).reshape(rows.shape)


def body(r, k, v, x, u, g, spans):
    tokens, width = r.shape
    npairs = width // LANES
    chips = lax.axis_size("chip")
    r, k, v, x, g, u = (hbm(part) for part in (r, k, v, x, g, u.reshape(1, -1)))
    spans = hbm(spans.reshape(1, -1))
    whole = pl.BlockSpec(memory_space=pltpu.VMEM)
    token = pl.BlockSpec(memory_space=pl.ANY)
    params = pltpu.CompilerParams(vmem_limit_bytes=VMEM)
    assert PAIRS == HALF

    def cost(flops, moved):
        return pl.CostEstimate(flops=flops, bytes_accessed=moved, transcendentals=0)

    def inside(half, after):
        part = INSIDE * LANES
        here = half * HALF // INSIDE
        wide = pl.BlockSpec((TOK, part), lambda i: (0, i + here))
        return pl.pallas_call(
            inside_kernel,
            grid=(HALF // INSIDE,),
            in_specs=[whole] + [wide] * 5 + [pl.BlockSpec((1, part), lambda i: (0, i + here)), token],
            out_specs=[
                pl.BlockSpec((FULL_TOK + 8, part), lambda i: (0, i)),
                pl.BlockSpec((4 * TOK, part), lambda i: (0, i)),
                pl.BlockSpec((8, LANES), lambda i: (0, 0)),
            ],
            out_shape=[
                pltpu.HBM((FULL_TOK + 8, HALF * LANES), F32),
                (pltpu.VMEM if half else pltpu.HBM)((4 * TOK, HALF * LANES), BF16),
                pltpu.HBM((8, LANES), F32),
            ],
            scratch_shapes=[pltpu.VMEM((TOK, part), F32), pltpu.VMEM((4, TOK, LANES), F32)],
            name="inside",
            compiler_params=params,
            cost_estimate=cost(10**10, 10**7),
        )(spans, r, k, v, g, x, u, hbm(after))

    part = PAIRS * LANES
    block = (BONUS + HALF, LANES)
    mine, theirs = pl.pallas_call(
        summary_kernel,
        grid=(width // part,),
        in_specs=[whole] + [pl.BlockSpec((TOK, part), lambda i: (0, i))] * 5,
        out_specs=[whole] * 2,
        out_shape=[jax.ShapeDtypeStruct(block, F32)] * 2,
        scratch_shapes=[
            pltpu.VMEM((TOK, part), F32),
            pltpu.VMEM((4, TOK, LANES), F32),
            pltpu.VMEM(block, F32),
        ],
        name="summary",
        compiler_params=params,
        cost_estimate=cost(10**9, 6 * 10**6),
    )(spans, r, k, v, g, x)
    theirs = swap(theirs)
    packets, combined = pl.pallas_call(
        combine_kernel,
        in_specs=[whole] * 2,
        out_specs=[whole, whole],
        out_shape=[jax.ShapeDtypeStruct((chips * ROWS_OUT, LANES), F32), pltpu.HBM((8, LANES), F32)],
        name="combine",
        compiler_params=params,
        cost_estimate=cost(10**6, 2 * 10**6),
    )(mine, theirs)
    got = exchange(packets, chips, "chip")
    *first, done = inside(0, combined)
    states, scanned = pl.pallas_call(
        scan_kernel,
        in_specs=[whole, token],
        out_specs=[whole, whole],
        out_shape=[jax.ShapeDtypeStruct((chips * ROWS_BACK, LANES), F32), pltpu.HBM((8, LANES), F32)],
        name="scan",
        compiler_params=params,
        cost_estimate=cost(10**10, 3 * 10**7),
    )(vm(got), hbm(done))
    returned = exchange(states, chips, "chip")
    *second, done = inside(1, scanned)
    own, other = pl.pallas_call(
        expand_kernel,
        in_specs=[whole, whole, whole, token],
        out_specs=[whole] * 2,
        out_shape=[jax.ShapeDtypeStruct((BONUS, LANES), F32)] * 2,
        name="expand",
        compiler_params=params,
        cost_estimate=cost(10**10, 3 * 10**7),
    )(returned, mine, theirs, hbm(done))
    other = swap(other)
    dr, dk, dv, dx, du = pl.pallas_call(
        final_kernel,
        in_specs=[whole] * 6,
        out_specs=[pl.BlockSpec(memory_space=pl.ANY)] * 4 + [whole],
        out_shape=[pltpu.HBM((tokens, width), BF16)] * 4 + [jax.ShapeDtypeStruct((1, width), F32)],
        scratch_shapes=[
            pltpu.VMEM((4, tokens, width), BF16),
            pltpu.SemaphoreType.DMA((npairs // WRITE, 4)),
        ],
        name="final",
        compiler_params=params,
        cost_estimate=cost(10**9, 10**7),
    )(*(vm(part) for part in (*first, *second, own, other)))
    return dr, dk, dv, dx, du.reshape(width)


def solution(mesh):
    chips = Mesh(mesh.devices.reshape(-1, CORES), ("chip", "core"))
    split, whole = P(("chip", "core"), None), P()
    return jax.shard_map(
        body,
        mesh=chips,
        in_specs=(split, split, split, split, whole, split, whole),
        out_specs=(split, split, split, split, whole),
        check_vma=False,
    )
```
